128 devices in a mesh: seq: 8 (over y, core), enc: 16 (over z, x).
Axes of the slice: x: 4, y: 4, z: 4, core: 2. Of those that a mesh axis runs over, the one named last changes fastest.
Arguments:
- text: bfloat16 [10240, 4096], P('seq', 'enc'), may hold values from -16 to 16
- visual: bfloat16 [5120, 4096], P(('seq', 'enc')), may hold values from -6 to 6
- gain: bfloat16 [4096], P('enc'), may hold values from 0.25 to 1.75
- w_query: bfloat16 [4096, 4096], P('enc'), may hold values from -1 to 1
- w_keyval: bfloat16 [4096, 2048], P('enc'), may hold values from -1 to 1
- image_count: int32 [32], replicated, may hold values from 1 to 256, 5120 in all
- text_gap: int32 [33], replicated, may hold values from 1 to 256, 5120 in all
Outputs:
- attended: bfloat16 [10240, 4096], P('seq', 'enc')
The draws below stay inside these ranges and needn't reach their ends.
Inputs may be any that keep to these rules, and one draw needn't show every extreme that they name: `image_count`: 32 counts that sum to 5120; the largest is exactly 256. `text_gap`: 33 text runs that sum to 5120; the largest is exactly 256.
All inputs are finite; a program needn't handle non-finite values.
Results may differ from the reference program's by a relative error of at most 0.025.
Values may be sent and summed in bfloat16 or wider, within the bound.
A program may use at most 256 MiB of HBM per device.

```python
import math
import jax
import jax.numpy as jnp
import numpy as np
from jax import lax

D = 4096
NH = 32
KVH = 8
HD = 128
IMAGES = 32
MOST = 256
LEN = 10240
NVIS = 5120
VIS_DEV = 40
N_SEQ = 8
N_ENC = 16


def draw_text(key, part):
    noise_key = jax.random.fold_in(key, 11)
    noise = jnp.clip(jax.random.normal(noise_key, (LEN, D), jnp.float32), -6.0, 6.0)
    return noise.astype(jnp.bfloat16)


def projection_draw(key, columns):
    base_key = jax.random.fold_in(key, 21)
    base = jnp.clip(jax.random.normal(base_key, (D, columns), jnp.float32), -6.0, 6.0)
    return (base * D ** (-0.5)).astype(jnp.bfloat16)


def draw_w_query(key, part):
    return projection_draw(key, NH * HD)


def draw_w_keyval(key, part):
    base_key = jax.random.fold_in(key, 41)
    base = jnp.clip(jax.random.normal(base_key, (D, 2 * KVH * HD), jnp.float32), -6.0, 6.0)
    return (base * D ** (-0.5)).astype(jnp.bfloat16)


def levels(key, shape, cuts, low, top_value):
    level, own = 1.0, jax.random.fold_in(key, 6)
    for dim, shards_of in cuts:
        heights = jnp.exp(jax.random.uniform(jax.random.fold_in(own, dim), (shards_of,), jnp.float32, low / len(cuts), top_value / len(cuts)))
        level = level * jnp.repeat(heights, shape[dim] // shards_of).reshape([-1 if axis == dim else 1 for axis in range(len(shape))])
    return level


def profile(amount, total, bound, lean):
    loads = [(1 << 20) // math.isqrt(grade ** lean) + 1 for grade in range(2, amount + 1)]
    rest, given = total - bound - (amount - 1), [1] * (amount - 1)
    while rest > 0:
        free = [i for i in range(amount - 1) if given[i] < bound]
        mass, remaining = sum([loads[i] for i in free]), rest
        for i in free:
            addition = min(bound - given[i], max(1, remaining * loads[i] // mass), rest)
            given[i] = given[i] + addition
            rest = rest - addition
    return np.array([bound] + given)


def uneven_parts(key, amount, total, limit, skew):
    if amount == 2:
        one = jax.random.randint(key, (), max(1, total - limit), min(limit, total - 1) + 1)
        return jnp.stack([one, total - one])
    lengths = jnp.asarray(profile(amount, total, limit, skew), jnp.int32)
    twos = (amount - 1) // 2
    source_of, receiver = lengths[1:1 + 2 * twos:2], lengths[2:2 + 2 * twos:2]
    margin = jnp.minimum(source_of - 1, limit - receiver)
    moved = jax.random.randint(jax.random.fold_in(key, 1), (twos,), 0, 1 << 20) % (margin + 1)
    lengths = lengths.at[1:1 + 2 * twos:2].set(source_of - moved).at[2:2 + 2 * twos:2].set(receiver + moved)
    return lengths[jax.random.permutation(jax.random.fold_in(key, 2), amount)]


def gaussian(rng, dims, spread, reach, split=(), kind=jnp.bfloat16):
    drawn = spread * jax.random.normal(rng, dims, jnp.float32)
    if split:
        drawn = drawn * levels(rng, dims, split, -0.22, 0.18)
    return jnp.clip(drawn, -reach, reach).astype(kind)


def setup_inputs(seed: int = 0) -> dict:
    streams_of = jax.random.split(jax.random.key(seed), 8)
    text = draw_text(jax.random.fold_in(streams_of[7], 71), 0)
    visual = gaussian(streams_of[1], (NVIS, D), 1.0, 6.0, ((0, 128),))
    gain = jnp.clip(1.0 + 0.15 * jax.random.normal(streams_of[2], (D,), jnp.float32), 0.25, 1.75).astype(jnp.bfloat16)
    w_query = draw_w_query(jax.random.fold_in(streams_of[7], 71), 0)
    w_keyval = draw_w_keyval(jax.random.fold_in(streams_of[7], 71), 0)
    image_count = uneven_parts(streams_of[5], IMAGES, NVIS, MOST, 2).astype(jnp.int32)
    text_gap = uneven_parts(streams_of[6], IMAGES + 1, LEN - NVIS, MOST, 2).astype(jnp.int32)
    return {"text": text, "visual": visual, "gain": gain, "w_query": w_query, "w_keyval": w_keyval, "image_count": image_count, "text_gap": text_gap}


eps = 1e-05

def layout(image_count, text_gap):
    counts = image_count.astype(jnp.int32)
    offsets = jnp.cumsum(counts) - counts
    starts = jnp.cumsum(text_gap[:-1]).astype(jnp.int32) + offsets
    return (offsets, starts)

def reference(text, visual, gain, w_query, w_keyval, image_count, text_gap):
    offsets, starts = layout(image_count, text_gap)
    span_ends = starts + image_count
    positions = jnp.arange(LEN, dtype=jnp.int32)
    inside = (positions[:, None] >= starts[None, :]) & (positions[:, None] < span_ends[None, :])
    frame_ids = jnp.arange(IMAGES, dtype=jnp.int32) + 1
    span_of = lax.optimization_barrier(jnp.sum(jnp.where(inside, frame_ids[None, :], 0), axis=1)).astype(jnp.int32) - 1
    row_index = lax.optimization_barrier(jnp.sum(jnp.where(inside, (offsets - starts)[None, :], 0), axis=1)).astype(jnp.int32) + positions
    is_visual = span_of >= 0
    device_total = N_SEQ * N_ENC
    token_index = jnp.where(is_visual, row_index, 0).astype(jnp.int32)
    stored_row = (token_index % device_total * VIS_DEV + token_index // device_total).astype(jnp.int32)
    picked = jnp.take(visual, stored_row, axis=0)
    stream = jnp.where(is_visual[:, None], picked, text)
    widened = stream.astype(jnp.float32)
    mean_square = lax.optimization_barrier(jnp.mean(widened * widened, axis=1, keepdims=True))
    normed = (widened * lax.rsqrt(mean_square + eps) * gain.astype(jnp.float32)[None, :]).astype(jnp.bfloat16)
    query = jnp.dot(normed, w_query, preferred_element_type=jnp.float32).astype(jnp.bfloat16)
    keyval = jnp.dot(normed, w_keyval, preferred_element_type=jnp.float32).astype(jnp.bfloat16)
    keyval = keyval.reshape(LEN, KVH, 2, HD)
    group_size = NH // KVH
    query_rows = min(512, LEN)
    score_scale = 1.0 / HD ** 0.5

    def head_output(head_id):
        query_head = lax.dynamic_slice_in_dim(query, head_id * HD, HD, 1)
        kv_head = lax.dynamic_index_in_dim(keyval, head_id // group_size, 1, keepdims=False)
        key_part = kv_head[:, 0, :]
        value_part = kv_head[:, 1, :]

        def block_output(first_row):
            query_block = lax.dynamic_slice_in_dim(query_head, first_row, query_rows, 0)
            scores = jnp.dot(query_block, key_part.T, preferred_element_type=jnp.float32) * score_scale
            query_pos = first_row + jnp.arange(query_rows, dtype=jnp.int32)
            query_span = lax.dynamic_slice_in_dim(span_of, first_row, query_rows, 0)
            visible = (positions[None, :] <= query_pos[:, None]) | (query_span[:, None] == span_of[None, :]) & (query_span[:, None] >= 0)
            masked = jnp.where(visible, scores, -1e+30)
            row_max = lax.optimization_barrier(jnp.max(masked, axis=1, keepdims=True))
            weights = jnp.where(visible, jnp.exp(masked - row_max), 0.0)
            totals = lax.optimization_barrier(jnp.sum(weights, axis=1, keepdims=True))
            probs = weights.astype(jnp.bfloat16)
            result = jnp.dot(probs, value_part, preferred_element_type=jnp.float32) / totals
            return result.astype(jnp.bfloat16)
        starts_rows = jnp.arange(LEN // query_rows, dtype=jnp.int32) * query_rows
        return lax.map(block_output, starts_rows).reshape(LEN, HD)
    outputs = lax.map(head_output, jnp.arange(NH, dtype=jnp.int32))
    return jnp.transpose(outputs, (1, 0, 2)).reshape(LEN, NH * HD)
```

```python
import functools
import math

import jax
import jax.numpy as jnp
from jax import lax
from jax.experimental import pallas as pl
from jax.experimental.pallas import tpu as pltpu
from jax.sharding import PartitionSpec as P

HD = 128
EPS = 1e-05
WINDOW = 16
NEG = -1e30
SAFE = 64.0
VMEM = pltpu.VMEM


def layout(image_count, text_gap):
    offsets = jnp.cumsum(image_count) - image_count
    starts = jnp.cumsum(text_gap[:-1]) + offsets
    return (offsets, starts)


def assemble_kernel(tile, index_ref, text_ref, arrived_ref, out_ref):
    slots = arrived_ref.shape[0]

    @pl.loop(0, text_ref.shape[0] // tile)
    def _(step):
        rows = pl.ds(pl.multiple_of(step * tile, tile), tile)
        index = index_ref[rows, :]
        lanes = lax.broadcasted_iota(jnp.int32, (tile, slots), 1)
        chosen = jnp.where(lanes == index, 1.0, 0.0).astype(jnp.bfloat16)
        picked = jnp.dot(chosen, arrived_ref[...], preferred_element_type=jnp.float32)
        out_ref[rows, :] = jnp.where(index >= 0, picked.astype(jnp.bfloat16), text_ref[rows, :])


def assemble(index, text, arrived):
    return pl.pallas_call(
        functools.partial(assemble_kernel, 128),
        out_shape=jax.ShapeDtypeStruct(text.shape, text.dtype),
        in_specs=[pl.BlockSpec(memory_space=VMEM)] * 3,
        out_specs=pl.BlockSpec(memory_space=VMEM),
    )(index, text, arrived)


def attention_kernel(bq, bk, sbq, sbk, off_ref, q_ref, kv_ref, lim_ref, o_ref, acc, den, top):
    heads = q_ref.shape[1] // HD
    rows_all, keys_all = q_ref.shape[0], kv_ref.shape[0]
    q0 = off_ref[0]

    def query_norm(step, best):
        block = q_ref[pl.ds(pl.multiple_of(step * 128, 128), 128), :].astype(jnp.float32)
        square = block * block
        for head in range(heads):
            norm = jnp.sum(square[:, head * HD : (head + 1) * HD], axis=1, keepdims=True)
            best = jnp.maximum(best, norm)
        return best

    def key_norm(step, best):
        block = kv_ref[pl.ds(pl.multiple_of(step * 128, 128), 128), :HD].astype(jnp.float32)
        return jnp.maximum(best, jnp.sum(block * block, axis=1, keepdims=True))

    zero = jnp.zeros((128, 1), jnp.float32)
    largest_query = jnp.max(lax.fori_loop(0, rows_all // 128, query_norm, zero))
    largest_key = jnp.max(lax.fori_loop(0, keys_all // 128, key_norm, zero))
    safe = largest_query * largest_key < SAFE * SAFE

    def scores(row, head, size, key, count, masked):
        q = q_ref[pl.ds(row, size), head * HD : (head + 1) * HD]
        s = lax.dot_general(
            q,
            kv_ref[pl.ds(key, count), :HD],
            (((1,), (1,)), ((), ())),
            preferred_element_type=jnp.float32,
        )
        if masked:
            at = key + lax.broadcasted_iota(jnp.int32, (size, count), 1)
            s = jnp.where(at <= lim_ref[pl.ds(row, size), :], s, NEG)
        return s

    def lane_sums(p):
        total = p[:, :HD]
        for part in range(1, p.shape[1] // HD):
            total = total + p[:, part * HD : (part + 1) * HD]
        return total

    def tiles(size, count, begin, step, end):
        @pl.loop(0, rows_all // size)
        def _(tile):
            row = pl.multiple_of(tile * size, size)
            begin()
            first = q0 + row
            whole = first // count
            last = jnp.minimum(pl.cdiv(first + size + 255, count), keys_all // count)

            @pl.loop(0, whole)
            def _(j):
                step(row, pl.multiple_of(j * count, count), False)

            @pl.loop(whole, last)
            def _(j):
                step(row, pl.multiple_of(j * count, count), True)

            end(row)

    @pl.when(safe)
    def _():
        def begin():
            acc[...] = jnp.zeros_like(acc)
            den[...] = jnp.zeros_like(den)

        def step(row, key, masked):
            values = kv_ref[pl.ds(key, bk), HD:]
            for head in range(heads):
                p = jnp.exp2(scores(row, head, bq, key, bk, masked))
                acc[head] += jnp.dot(
                    p.astype(jnp.bfloat16), values, preferred_element_type=jnp.float32
                )
                den[head] += lane_sums(p)

        def end(row):
            for head in range(heads):
                result = acc[head] / jnp.sum(den[head], axis=1, keepdims=True)
                o_ref[pl.ds(row, bq), head * HD : (head + 1) * HD] = result.astype(jnp.bfloat16)

        tiles(bq, bk, begin, step, end)

    @pl.when(jnp.logical_not(safe))
    def _():
        part = pl.ds(0, sbq)

        def begin():
            acc[...] = jnp.zeros_like(acc)
            den[...] = jnp.zeros_like(den)
            top[...] = jnp.full_like(top, NEG)

        def step(row, key, masked):
            values = kv_ref[pl.ds(key, sbk), HD:]
            for head in range(heads):
                s = scores(row, head, sbq, key, sbk, masked)
                old = top[head]
                new = jnp.maximum(old, jnp.max(s, axis=1, keepdims=True))
                top[head] = new
                p = jnp.exp2(s - new)
                shrink = jnp.exp2(old - new)
                acc[head, part] = acc[head, part] * shrink + jnp.dot(
                    p.astype(jnp.bfloat16), values, preferred_element_type=jnp.float32
                )
                den[head, part] = den[head, part] * shrink + lane_sums(p)

        def end(row):
            for head in range(heads):
                result = acc[head, part] / jnp.sum(den[head, part], axis=1, keepdims=True)
                o_ref[pl.ds(row, sbq), head * HD : (head + 1) * HD] = result.astype(jnp.bfloat16)

        tiles(sbq, sbk, begin, step, end)


def attention(q0, query, keyval, lim):
    rows, width = query.shape
    heads = width // HD
    bq, bk, sbq, sbk = rows // 2, 1024, 128, 512
    flops = 4 * rows * keyval.shape[0] * width
    return pl.pallas_call(
        functools.partial(attention_kernel, bq, bk, sbq, sbk),
        out_shape=jax.ShapeDtypeStruct(query.shape, jnp.bfloat16),
        in_specs=[pl.BlockSpec(memory_space=pltpu.SMEM)] + [pl.BlockSpec(memory_space=VMEM)] * 3,
        out_specs=pl.BlockSpec(memory_space=VMEM),
        scratch_shapes=[
            VMEM((heads, bq, HD), jnp.float32),
            VMEM((heads, bq, HD), jnp.float32),
            VMEM((heads, sbq, 1), jnp.float32),
        ],
        compiler_params=pltpu.CompilerParams(vmem_limit_bytes=56 << 20),
        cost_estimate=pl.CostEstimate(
            flops=flops, bytes_accessed=keyval.size * 2, transcendentals=rows * keyval.shape[0]
        ),
    )(q0, query, keyval, lim)


def per_device(text, visual, gain, w_query, w_keyval, image_count, text_gap):
    rows, features = text.shape
    vis_rows = visual.shape[0]
    seq_count, enc_count = lax.axis_size("seq"), lax.axis_size("enc")
    seq_index, enc_index = lax.axis_index("seq"), lax.axis_index("enc")
    device_total = seq_count * enc_count
    side = math.isqrt(enc_count)
    near = [[z * side + x for x in range(side)] for z in range(side)]
    far = [[z * side + x for z in range(side)] for x in range(side)]

    w = jnp.concatenate(
        (
            w_query.reshape(features, side, side, -1),
            w_keyval.reshape(features, side, side, -1),
        ),
        axis=3,
    )
    columns = w.shape[3]
    q_columns = w_query.shape[1] // enc_count
    w = (w.astype(jnp.float32) * gain.astype(jnp.float32)[:, None, None, None]).astype(jnp.bfloat16)
    w = jnp.transpose(w, (2, 0, 1, 3)).reshape(side, features, side * columns)
    w = lax.all_to_all(w, "enc", split_axis=0, concat_axis=0, axis_index_groups=near, tiled=True)
    w = w.reshape(side * features, side * columns)

    offsets, starts = layout(image_count, text_gap)
    ends = starts + image_count
    edges = jnp.arange(seq_count, dtype=jnp.int32) * rows
    before = jnp.sum(
        jnp.clip(edges[:, None] - starts[None, :], 0, image_count[None, :]), axis=1
    ).astype(jnp.int32)
    first_row = jnp.minimum(before // device_total, vis_rows - WINDOW)
    pieces = jnp.stack(
        [lax.dynamic_slice_in_dim(visual, first_row[s], WINDOW, 0) for s in range(seq_count)]
    )
    pieces = pieces.reshape(seq_count, WINDOW, enc_count, features)
    pieces = jnp.transpose(pieces, (0, 2, 1, 3)).reshape(device_total, WINDOW, features)
    arrived = lax.all_to_all(pieces, ("seq", "enc"), split_axis=0, concat_axis=0, tiled=True)
    arrived = arrived.reshape(device_total * WINDOW, features)

    positions = seq_index * rows + jnp.arange(rows, dtype=jnp.int32)
    inside = (positions[:, None] >= starts[None, :]) & (positions[:, None] < ends[None, :])
    is_visual = jnp.any(inside, axis=1)
    token = jnp.sum(jnp.where(inside, (offsets - starts)[None, :], 0), axis=1) + positions
    slot = token % device_total * WINDOW + token // device_total - first_row[seq_index]
    index = jnp.where(is_visual, slot, -1).astype(jnp.int32)
    last_key = jnp.maximum(
        jnp.sum(jnp.where(inside, ends[None, :], 0), axis=1) - 1, positions
    ).astype(jnp.int32)
    stream = assemble(index[:, None], text, arrived)

    widened = stream.astype(jnp.float32)
    square = lax.psum(jnp.sum(widened * widened, axis=1), "enc")
    scale = lax.rsqrt(square / (features * enc_count) + EPS)[:, None]
    gathered = lax.all_gather(stream, "enc", axis=1, axis_index_groups=near, tiled=True)
    partial = jnp.dot(gathered, w, preferred_element_type=jnp.float32).astype(jnp.bfloat16)
    summed = lax.psum_scatter(
        partial, "enc", scatter_dimension=1, axis_index_groups=far, tiled=True
    ).astype(jnp.float32)
    query = (summed[:, :q_columns] * (scale * (math.log2(math.e) / HD**0.5))).astype(jnp.bfloat16)
    own = (summed[:, q_columns:] * scale).astype(jnp.bfloat16)
    partner = lax.ppermute(own, "enc", [(i, i ^ 1) for i in range(enc_count)])
    holds_keys = enc_index % 2 == 0
    keyval = jnp.concatenate(
        (jnp.where(holds_keys, own, partner), jnp.where(holds_keys, partner, own)), axis=1
    )
    keyval = lax.all_gather(keyval, "seq", axis=0, tiled=True)
    q0 = (seq_index * rows).astype(jnp.int32).reshape(1)
    return attention(q0, query, keyval, last_key[:, None])


def solution(mesh):
    in_specs = (
        P("seq", "enc"),
        P(("seq", "enc"), None),
        P("enc"),
        P("enc", None),
        P("enc", None),
        P(),
        P(),
    )
    out_specs = P("seq", "enc")
    return jax.shard_map(
        per_device, mesh=mesh, in_specs=in_specs, out_specs=out_specs, check_vma=False
    )
```

```python
import functools
import math

import jax
import jax.numpy as jnp
from jax import lax
from jax.experimental import pallas as pl
from jax.experimental.pallas import tpu as pltpu
from jax.sharding import PartitionSpec as P

HD = 128
EPS = 1e-05
CHUNK = 128
MESH = pl.DeviceIdType.MESH
NEG = -1e30
SAFE = 64.0
VMEM = pltpu.VMEM


def spread(row):
    return jnp.broadcast_to(row, (HD, HD)).T


def project_kernel(
    side, count_ref, gap_ref, text_ref, visual_ref, gain_ref, wq_ref, wkv_ref,
    q_out, kv_out, lim_out,
    before, wsend, wall, seen, picked, landed, slots, lims, xall, psend, precv, squares, sqrecv,
    vis_s, vis_r, blk_s, blk_r, w_s, w_r, wf_s, wf_r, x_s, x_r, p_s, p_r, n_s, n_r,
    kx_s, kx_r, ky_s, ky_r, kc_s, kc_r,
):
    seq_count, enc_count = lax.axis_size("seq"), lax.axis_size("enc")
    s, e = lax.axis_index("seq"), lax.axis_index("enc")
    y, core, z, x = s // 2, s % 2, e // side, e % side
    ys = seq_count // 2
    rows, features = text_ref.shape
    chunks = rows // CHUNK
    window = landed.shape[1]
    vis_rows = seen.shape[1]
    columns = psend.shape[2]
    q_columns = q_out.shape[1]
    k_columns = columns - q_columns
    half = wall.shape[2] // 2
    images = count_ref.shape[0]
    twin = s + 1 - 2 * core
    mate = e + 1 - 2 * (e % 2)

    def across(k):
        return z * side + (x + k) % side

    def along(k):
        return ((z + k) % side) * side + x

    def column_of(k):
        return ((y + k) % ys) * 2 + core

    def send(source, target, ssem, rsem, to_s, to_e):
        return pltpu.make_async_remote_copy(
            src_ref=source, dst_ref=target, send_sem=ssem, recv_sem=rsem,
            device_id=(to_s, to_e), device_id_type=MESH,
        )

    barrier = pltpu.get_barrier_semaphore()

    @pl.loop(1, enc_count)
    def _(k):
        pl.semaphore_signal(barrier, inc=1, device_id=(s, (e + k) % enc_count), device_id_type=MESH)

    @pl.loop(1, seq_count)
    def _(k):
        pl.semaphore_signal(barrier, inc=1, device_id=((s + k) % seq_count, e), device_id_type=MESH)

    pl.semaphore_wait(barrier, enc_count + seq_count - 2)

    def see(k):
        to = (e + k) % enc_count
        lanes = pl.ds(pl.multiple_of(to * features, features), features)
        return send(visual_ref.at[:, lanes], seen.at[e], vis_s.at[k], vis_r.at[k], s, to)

    @pl.loop(1, enc_count)
    def _(k):
        see(k).start()

    seen[e] = visual_ref[:, pl.ds(pl.multiple_of(e * features, features), features)]

    gains = [
        spread(gain_ref[:, g * HD : (g + 1) * HD].astype(jnp.float32)) for g in range(features // HD)
    ]

    def scaled(ref, part, start):
        lanes = pl.ds(pl.multiple_of(start, HD), HD)
        block = ref[part * HD : (part + 1) * HD, lanes].astype(jnp.float32)
        return (block * gains[part]).astype(jnp.bfloat16)

    @pl.loop(0, side)
    def _(to):
        for zz in range(side):
            for part in range(features // HD):
                there = pl.ds(part * HD, HD)
                owner = zz * side + to
                for j in range(q_columns // HD):
                    wsend[to, there, pl.ds(zz * columns + j * HD, HD)] = scaled(
                        wq_ref, part, owner * q_columns + j * HD
                    )
                for j in range(k_columns // HD):
                    wsend[to, there, pl.ds(zz * columns + q_columns + j * HD, HD)] = scaled(
                        wkv_ref, part, owner * k_columns + j * HD
                    )

    mine = pl.ds(pl.multiple_of(core * half, HD), half)

    def weigh(k):
        return send(
            wsend.at[(x + k) % side, :, mine], wall.at[x, :, mine],
            w_s.at[k], w_r.at[k], s, across(k),
        )

    def pass_weights(k):
        origin = (x + side - k) % side
        return send(
            wall.at[origin, :, mine], wall.at[origin, :, mine], wf_s.at[k], wf_r.at[k], twin, e
        )

    @pl.loop(1, side)
    def _(k):
        weigh(k).start()

    wall[x] = wsend[x]

    shape = slots.shape
    position = (
        s * rows
        + lax.broadcasted_iota(jnp.int32, shape, 0) * CHUNK
        + lax.broadcasted_iota(jnp.int32, shape, 1)
    )

    def place(i, carry):
        end, offset, shift, lim, counts = carry
        start = end + gap_ref[i]
        count = count_ref[i]
        end = start + count
        inside = (position >= start) & (position < end)
        shift = jnp.where(inside, offset - start, shift)
        lim = jnp.where(inside, end - 1, lim)
        counts = tuple(
            total + jnp.minimum(jnp.maximum(b * rows - start, 0), count)
            for b, total in enumerate(counts)
        )
        return end, offset + count, shift, lim, counts

    none = jnp.full(shape, 1, jnp.int32)
    zero = jnp.int32(0)
    _, _, shift, lim, counts = lax.fori_loop(
        0, images, place, (zero, zero, none, position, (zero,) * seq_count)
    )
    for b in range(seq_count):
        before[b] = counts[b]
    lims[...] = lim.astype(jnp.float32)
    token = position + shift
    origin = (token // enc_count) % seq_count
    total = before[s]
    group = seq_count * enc_count
    skipped = (total // group) * enc_count + jnp.clip(total % group - enc_count * origin, 0, enc_count)
    slot = origin * window + (token // group) * enc_count + token % enc_count - skipped
    slots[...] = jnp.where(shift <= 0, slot, -1).astype(jnp.float32)

    @pl.loop(1, enc_count)
    def _(k):
        see(k).wait_recv()

    def one_hot(index, count):
        lane = lax.broadcasted_iota(jnp.int32, index.shape, 1).astype(jnp.float32)
        return jnp.concatenate(
            [jnp.where(index == lane + j * HD, 1.0, 0.0).astype(jnp.bfloat16) for j in range(count // HD)],
            axis=1,
        )

    def pick(b):
        total = before[b]
        skip = (total // group) * enc_count + jnp.clip(total % group - enc_count * s, 0, enc_count)
        local = skip + lax.broadcasted_iota(jnp.int32, (window, HD), 0)
        index = (local % enc_count) * vis_rows + local // enc_count
        chosen = one_hot(index.astype(jnp.float32), enc_count * vis_rows)
        table = seen[...].reshape(enc_count * vis_rows, features)
        return jnp.dot(chosen, table, preferred_element_type=jnp.float32).astype(jnp.bfloat16)

    def move(k):
        to = (s + k) % seq_count
        return send(picked.at[to], landed.at[s], blk_s.at[k], blk_r.at[k], to, e)

    @pl.loop(1, seq_count)
    def _(k):
        to = (s + k) % seq_count
        picked[to] = pick(to)
        move(k).start()

    landed[s] = pick(s)

    @pl.loop(1, side)
    def _(k):
        weigh(k).wait_recv()
        pass_weights(k).start()

    @pl.loop(1, seq_count)
    def _(k):
        move(k).wait_recv()

    def at(c):
        return pl.ds(pl.multiple_of(c * CHUNK, CHUNK), CHUNK)

    def share(k, c):
        return send(xall.at[x, at(c)], xall.at[x, at(c)], x_s.at[k, c], x_r.at[k, c], s, across(k))

    @pl.loop(0, chunks)
    def _(c):
        index = spread(slots[pl.ds(c, 1), :])
        chosen = one_hot(index, landed.shape[0] * window)
        table = landed[...].reshape(landed.shape[0] * window, features)
        frame = jnp.dot(chosen, table, preferred_element_type=jnp.float32).astype(jnp.bfloat16)
        visual = jnp.concatenate([index] * (features // HD), axis=1) >= 0
        xall[x, at(c)] = jnp.where(visual, frame, text_ref[at(c), :])
        lim_out[at(c), :] = spread(lims[pl.ds(c, 1), :])
        for k in range(1, side):
            share(k, c).start()

    @pl.loop(1, side)
    def _(k):
        pass_weights(k).wait_recv()

    def reduce(k, c):
        return send(
            psend.at[(z + k) % side, at(c)], precv.at[k, at(c)],
            p_s.at[k, c], p_r.at[k, c], s, along(k),
        )

    def norms(k, c):
        return send(squares.at[c], sqrecv.at[k, c], n_s.at[k, c], n_r.at[k, c], s, along(k))

    def keys(owner, c):
        return pl.ds(pl.multiple_of(owner * rows + c * CHUNK, CHUNK), CHUNK)

    def pair(c):
        here = kv_out.at[e % 2, keys(s, c)]
        return send(here, here, kx_s.at[c], kx_r.at[c], s, mate)

    def column(k, c):
        here = kv_out.at[:, keys(s, c)]
        return send(here, here, ky_s.at[k, c], ky_r.at[k, c], column_of(k), e)

    def chip(k, c):
        here = kv_out.at[:, keys(column_of(ys - k), c)]
        return send(here, here, kc_s.at[k, c], kc_r.at[k, c], twin, e)

    ones = jnp.ones((8, side * features), jnp.bfloat16)

    def multiply(c):
        for k in range(1, side):
            share(k, c).wait_recv()
        block = jnp.concatenate([xall[j, at(c)] for j in range(side)], axis=1)
        wide = block.astype(jnp.float32)
        squares[c] = lax.dot_general(
            ones, (wide * wide).astype(jnp.bfloat16), (((1,), (1,)), ((), ())),
            preferred_element_type=jnp.float32,
        )
        for k in range(1, side):
            norms(k, c).start()
        weights = wall[...].reshape(side * features, side * columns)
        partial = jnp.dot(block, weights, preferred_element_type=jnp.float32).astype(jnp.bfloat16)
        for zz in range(side):
            psend[zz, at(c)] = partial[:, zz * columns : (zz + 1) * columns]
        for k in range(1, side):
            reduce(k, c).start()

    def finish(c):
        total = psend[z, at(c)].astype(jnp.float32)
        square = squares[c]
        for k in range(1, side):
            reduce(k, c).wait_recv()
            norms(k, c).wait_recv()
            total = total + precv[k, at(c)].astype(jnp.float32)
            square = square + sqrecv[k, c]
        scale = spread(lax.rsqrt(square / (features * enc_count) + EPS)[0:1, :])
        factor = math.log2(math.e) / HD**0.5
        for j in range(q_columns // HD):
            lanes = slice(j * HD, (j + 1) * HD)
            q_out[at(c), lanes] = (total[:, lanes] * (scale * factor)).astype(jnp.bfloat16)
        kv_out[e % 2, keys(s, c)] = (total[:, q_columns:] * scale).astype(jnp.bfloat16)
        pair(c).start()

    def spread_out(c):
        pair(c).wait_recv()
        for k in range(1, ys):
            column(k, c).start()
        chip(0, c).start()

    def hand_over(c):
        for k in range(1, ys):
            column(k, c).wait_recv()
            chip(k, c).start()

    stages = (multiply, finish, spread_out, hand_over)
    lags = (0, 1, 2, 4)

    @pl.loop(0, chunks + lags[-1])
    def _(t):
        for stage, lag in zip(stages, lags):
            @pl.when((t >= lag) & (t < chunks + lag))
            def _():
                stage(t - lag)

    @pl.loop(0, chunks)
    def _(c):
        pair(c).wait_send()
        chip(0, c).wait()
        for k in range(1, ys):
            chip(k, c).wait()
            column(k, c).wait_send()
        for k in range(1, side):
            share(k, c).wait_send()
            reduce(k, c).wait_send()
            norms(k, c).wait_send()

    @pl.loop(1, side)
    def _(k):
        weigh(k).wait_send()
        pass_weights(k).wait_send()

    @pl.loop(1, enc_count)
    def _(k):
        see(k).wait_send()

    @pl.loop(1, seq_count)
    def _(k):
        move(k).wait_send()


def project(text, visual, gain, w_query, w_keyval, image_count, text_gap):
    rows, features = text.shape
    vis_rows = visual.shape[0]
    seq_count, enc_count = lax.axis_size("seq"), lax.axis_size("enc")
    side, ys = math.isqrt(enc_count), seq_count // 2
    q_columns = w_query.shape[1] // enc_count
    columns = q_columns + w_keyval.shape[1] // enc_count
    chunks = rows // CHUNK
    window = rows // seq_count
    bf16, f32 = jnp.bfloat16, jnp.float32

    def dma(*shape):
        return [pltpu.SemaphoreType.DMA(shape)] * 2

    return pl.pallas_call(
        functools.partial(project_kernel, side),
        out_shape=(
            jax.ShapeDtypeStruct((rows, q_columns), bf16),
            jax.ShapeDtypeStruct((2, rows * seq_count, HD), bf16),
            jax.ShapeDtypeStruct((rows, HD), f32),
        ),
        in_specs=[pl.BlockSpec(memory_space=pltpu.SMEM)] * 2 + [pl.BlockSpec(memory_space=VMEM)] * 5,
        out_specs=tuple([pl.BlockSpec(memory_space=VMEM)] * 3),
        scratch_shapes=[
            pltpu.SMEM((seq_count,), jnp.int32),
            VMEM((side, features, side * columns), bf16),
            VMEM((side, features, side * columns), bf16),
            VMEM((enc_count, vis_rows, features), bf16),
            VMEM((seq_count, window, features), bf16),
            VMEM((seq_count, window, features), bf16),
            VMEM((16, HD), f32),
            VMEM((16, HD), f32),
            VMEM((side, rows, features), bf16),
            VMEM((side, rows, columns), bf16),
            VMEM((side, rows, columns), bf16),
            VMEM((chunks, 8, CHUNK), f32),
            VMEM((side, chunks, 8, CHUNK), f32),
            *dma(enc_count),
            *dma(seq_count),
            *dma(side),
            *dma(side),
            *dma(side, chunks),
            *dma(side, chunks),
            *dma(side, chunks),
            *dma(chunks),
            *dma(ys, chunks),
            *dma(ys, chunks),
        ],
        compiler_params=pltpu.CompilerParams(
            collective_id=0, has_side_effects=True, vmem_limit_bytes=60 << 20
        ),
    )(image_count, text_gap, text, visual, gain, w_query, w_keyval)


def attention_kernel(bq, bk, sbq, sbk, off_ref, q_ref, kv_ref, lim_ref, o_ref, acc, den, top):
    heads = q_ref.shape[1] // HD
    rows_all, keys_all = q_ref.shape[0], kv_ref.shape[1]
    q0 = off_ref[0]

    def query_norm(step, best):
        block = q_ref[pl.ds(pl.multiple_of(step * 128, 128), 128), :].astype(jnp.float32)
        square = block * block
        for head in range(heads):
            norm = jnp.sum(square[:, head * HD : (head + 1) * HD], axis=1, keepdims=True)
            best = jnp.maximum(best, norm)
        return best

    def key_norm(step, best):
        block = kv_ref[0, pl.ds(pl.multiple_of(step * 128, 128), 128), :].astype(jnp.float32)
        return jnp.maximum(best, jnp.sum(block * block, axis=1, keepdims=True))

    zero = jnp.zeros((128, 1), jnp.float32)
    largest_query = jnp.max(lax.fori_loop(0, rows_all // 128, query_norm, zero))
    largest_key = jnp.max(lax.fori_loop(0, keys_all // 128, key_norm, zero))
    safe = largest_query * largest_key < SAFE * SAFE

    def scores(row, head, size, key, count, masked):
        q = q_ref[pl.ds(row, size), head * HD : (head + 1) * HD]
        s = lax.dot_general(
            q,
            kv_ref[0, pl.ds(key, count), :],
            (((1,), (1,)), ((), ())),
            preferred_element_type=jnp.float32,
        )
        if masked:
            at = (key + lax.broadcasted_iota(jnp.int32, (size, count), 1)).astype(jnp.float32)
            lim = jnp.concatenate([lim_ref[pl.ds(row, size), :]] * (count // HD), axis=1)
            s = jnp.where(at <= lim, s, NEG)
        return s

    def lane_sums(p):
        total = p[:, :HD]
        for part in range(1, p.shape[1] // HD):
            total = total + p[:, part * HD : (part + 1) * HD]
        return total

    def tiles(size, count, begin, step, end):
        @pl.loop(0, rows_all // size)
        def _(tile):
            row = pl.multiple_of(tile * size, size)
            begin()
            first = q0 + row
            whole = first // count
            last = jnp.minimum(pl.cdiv(first + size + 255, count), keys_all // count)

            @pl.loop(0, whole)
            def _(j):
                step(row, pl.multiple_of(j * count, count), False)

            @pl.loop(whole, last)
            def _(j):
                step(row, pl.multiple_of(j * count, count), True)

            end(row)

    @pl.when(safe)
    def _():
        def begin():
            acc[...] = jnp.zeros_like(acc)
            den[...] = jnp.zeros_like(den)

        def step(row, key, masked):
            values = kv_ref[1, pl.ds(key, bk), :]
            for head in range(heads):
                p = jnp.exp2(scores(row, head, bq, key, bk, masked))
                acc[head] += jnp.dot(
                    p.astype(jnp.bfloat16), values, preferred_element_type=jnp.float32
                )
                den[head] += lane_sums(p)

        def end(row):
            for head in range(heads):
                result = acc[head] / jnp.sum(den[head], axis=1, keepdims=True)
                o_ref[pl.ds(row, bq), head * HD : (head + 1) * HD] = result.astype(jnp.bfloat16)

        tiles(bq, bk, begin, step, end)

    @pl.when(jnp.logical_not(safe))
    def _():
        part = pl.ds(0, sbq)

        def begin():
            acc[...] = jnp.zeros_like(acc)
            den[...] = jnp.zeros_like(den)
            top[...] = jnp.full_like(top, NEG)

        def step(row, key, masked):
            values = kv_ref[1, pl.ds(key, sbk), :]
            for head in range(heads):
                s = scores(row, head, sbq, key, sbk, masked)
                old = top[head]
                new = jnp.maximum(old, jnp.max(s, axis=1, keepdims=True))
                top[head] = new
                p = jnp.exp2(s - new)
                shrink = jnp.exp2(old - new)
                acc[head, part] = acc[head, part] * shrink + jnp.dot(
                    p.astype(jnp.bfloat16), values, preferred_element_type=jnp.float32
                )
                den[head, part] = den[head, part] * shrink + lane_sums(p)

        def end(row):
            for head in range(heads):
                result = acc[head, part] / jnp.sum(den[head, part], axis=1, keepdims=True)
                o_ref[pl.ds(row, sbq), head * HD : (head + 1) * HD] = result.astype(jnp.bfloat16)

        tiles(sbq, sbk, begin, step, end)


def attention(q0, query, keyval, lim):
    rows, width = query.shape
    heads = width // HD
    bq, bk, sbq, sbk = rows // 2, 1024, 128, 512
    flops = 4 * rows * keyval.shape[1] * width
    return pl.pallas_call(
        functools.partial(attention_kernel, bq, bk, sbq, sbk),
        out_shape=jax.ShapeDtypeStruct(query.shape, jnp.bfloat16),
        in_specs=[pl.BlockSpec(memory_space=pltpu.SMEM)] + [pl.BlockSpec(memory_space=VMEM)] * 3,
        out_specs=pl.BlockSpec(memory_space=VMEM),
        scratch_shapes=[
            VMEM((heads, bq, HD), jnp.float32),
            VMEM((heads, bq, HD), jnp.float32),
            VMEM((heads, sbq, 1), jnp.float32),
        ],
        compiler_params=pltpu.CompilerParams(vmem_limit_bytes=56 << 20),
        cost_estimate=pl.CostEstimate(
            flops=flops, bytes_accessed=keyval.size * 2, transcendentals=rows * keyval.shape[1]
        ),
    )(q0, query, keyval, lim)


def per_device(text, visual, gain, w_query, w_keyval, image_count, text_gap):
    rows = text.shape[0]
    visual = jnp.pad(visual, ((0, -visual.shape[0] % 16), (0, 0)))
    query, keyval, lim = project(
        text, visual, gain[None, :], w_query, w_keyval, image_count, text_gap
    )
    q0 = (lax.axis_index("seq") * rows).astype(jnp.int32).reshape(1)
    return attention(q0, query, keyval, lim)


def solution(mesh):
    in_specs = (
        P("seq", "enc"),
        P(("seq", "enc"), None),
        P("enc"),
        P("enc", None),
        P("enc", None),
        P(),
        P(),
    )
    out_specs = P("seq", "enc")
    return jax.shard_map(
        per_device, mesh=mesh, in_specs=in_specs, out_specs=out_specs, check_vma=False
    )
```

```python
import functools
import math

import jax
import jax.numpy as jnp
from jax import lax
from jax.experimental import pallas as pl
from jax.experimental.pallas import tpu as pltpu
from jax.sharding import PartitionSpec as P

HD = 128
EPS = 1e-05
CHUNK = 128
MESH = pl.DeviceIdType.MESH
NEG = -1e30
SAFE = 64.0
VMEM = pltpu.VMEM


def spread(row):
    return jnp.broadcast_to(row, (HD, HD)).T


def project_kernel(
    side, count_ref, gap_ref, text_ref, visual_ref, gain_ref, wq_ref, wkv_ref,
    q_out, kv_out, lim_out,
    before, wsend, wall, seen, picked, landed, slots, lims, xall, psend, pmid, precv, squares,
    sqrecv, qown,
    vis_s, vis_r, blk_s, blk_r, w_s, w_r, wf_s, wf_r, x_s, x_r, xf_s, xf_r, p_s, p_r, pf_s, pf_r,
    n_s, n_r, kx_s, kx_r, ky_s, ky_r, kc_s, kc_r, q_s, q_r,
):
    seq_count, enc_count = lax.axis_size("seq"), lax.axis_size("enc")
    s, e = lax.axis_index("seq"), lax.axis_index("enc")
    y, core, z, x = s // 2, s % 2, e // side, e % side
    ys = seq_count // 2
    rows, features = text_ref.shape
    chunks = rows // CHUNK
    window = landed.shape[1]
    vis_rows = seen.shape[1]
    columns = psend.shape[2]
    q_columns = q_out.shape[1]
    k_columns = columns - q_columns
    half = wall.shape[2] // 2
    images = count_ref.shape[0]
    twin = s + 1 - 2 * core
    mate = e + 1 - 2 * (e % 2)
    other = seq_count - 1 - s
    sides = (1, side - 1)

    def across(k):
        return z * side + (x + k) % side

    def along(k):
        return ((z + k) % side) * side + x

    def column_of(k):
        return ((y + k) % ys) * 2 + core

    def send(source, target, ssem, rsem, to_s, to_e):
        return pltpu.make_async_remote_copy(
            src_ref=source, dst_ref=target, send_sem=ssem, recv_sem=rsem,
            device_id=(to_s, to_e), device_id_type=MESH,
        )

    seen[...] = jnp.zeros_like(seen)
    barrier = pltpu.get_barrier_semaphore()

    @pl.loop(1, enc_count)
    def _(k):
        pl.semaphore_signal(barrier, inc=1, device_id=(s, (e + k) % enc_count), device_id_type=MESH)

    @pl.loop(1, seq_count)
    def _(k):
        pl.semaphore_signal(barrier, inc=1, device_id=((s + k) % seq_count, e), device_id_type=MESH)

    pl.semaphore_wait(barrier, enc_count + seq_count - 2)

    def see(k):
        to = (e + k) % enc_count
        lanes = pl.ds(pl.multiple_of(to * features, features), features)
        there = seen.at[e, pl.ds(0, visual_ref.shape[0])]
        return send(visual_ref.at[:, lanes], there, vis_s.at[k], vis_r.at[k], s, to)

    @pl.loop(1, enc_count)
    def _(k):
        see(k).start()

    kept = pltpu.make_async_copy(
        visual_ref.at[:, pl.ds(pl.multiple_of(e * features, features), features)],
        seen.at[e, pl.ds(0, visual_ref.shape[0])],
        vis_s.at[0],
    )
    kept.start()

    gains = [
        spread(gain_ref[g * HD : (g + 1) * HD].astype(jnp.float32).reshape(1, HD)) for g in range(features // HD)
    ]

    def scaled(ref, part, start):
        lanes = pl.ds(pl.multiple_of(start, HD), HD)
        block = ref[part * HD : (part + 1) * HD, lanes].astype(jnp.float32)
        return (block * gains[part]).astype(jnp.bfloat16)

    @pl.loop(0, side)
    def _(to):
        for zz in range(side):
            for part in range(features // HD):
                there = pl.ds(part * HD, HD)
                owner = zz * side + to
                for j in range(q_columns // HD):
                    wsend[to, there, pl.ds(zz * columns + j * HD, HD)] = scaled(
                        wq_ref, part, owner * q_columns + j * HD
                    )
                for j in range(k_columns // HD):
                    wsend[to, there, pl.ds(zz * columns + q_columns + j * HD, HD)] = scaled(
                        wkv_ref, part, owner * k_columns + j * HD
                    )

    mine = pl.ds(pl.multiple_of(core * half, HD), half)

    def weigh(k):
        return send(
            wsend.at[(x + k) % side, :, mine], wall.at[x, :, mine],
            w_s.at[k], w_r.at[k], s, across(k),
        )

    def pass_weights(k):
        origin = (x + side - k) % side
        return send(
            wall.at[origin, :, mine], wall.at[origin, :, mine], wf_s.at[k], wf_r.at[k], twin, e
        )

    @pl.loop(1, side)
    def _(k):
        weigh(k).start()

    wall[x] = wsend[x]

    shape = slots.shape
    position = (
        s * rows
        + lax.broadcasted_iota(jnp.int32, shape, 0) * CHUNK
        + lax.broadcasted_iota(jnp.int32, shape, 1)
    )

    seat = jnp.where(
        lax.broadcasted_iota(jnp.int32, shape, 0) >= chunks // 2, position, position + (other - s) * rows
    )

    def place(i, carry):
        end, offset, shift, lim, counts = carry
        start = end + gap_ref[i]
        count = count_ref[i]
        end = start + count
        inside = (position >= start) & (position < end)
        shift = jnp.where(inside, offset - start, shift)
        lim = jnp.where((seat >= start) & (seat < end), end - 1, lim)
        counts = tuple(
            total + jnp.minimum(jnp.maximum(b * rows - start, 0), count)
            for b, total in enumerate(counts)
        )
        return end, offset + count, shift, lim, counts

    none = jnp.full(shape, 1, jnp.int32)
    zero = jnp.int32(0)
    _, _, shift, lim, counts = lax.fori_loop(
        0, images, place, (zero, zero, none, seat, (zero,) * seq_count)
    )
    for b in range(seq_count):
        before[b] = counts[b]
    lims[...] = lim.astype(jnp.float32)
    token = position + shift
    origin = (token // enc_count) % seq_count
    total = before[s]
    group = seq_count * enc_count
    skipped = (total // group) * enc_count + jnp.clip(total % group - enc_count * origin, 0, enc_count)
    slot = origin * window + (token // group) * enc_count + token % enc_count - skipped
    slots[...] = jnp.where(shift <= 0, slot, -1).astype(jnp.float32)

    @pl.loop(1, enc_count)
    def _(k):
        see(k).wait_recv()

    kept.wait()

    def one_hot(index, count):
        lane = lax.broadcasted_iota(jnp.int32, index.shape, 1).astype(jnp.float32)
        return jnp.concatenate(
            [jnp.where(index == lane + j * HD, 1.0, 0.0).astype(jnp.bfloat16) for j in range(count // HD)],
            axis=1,
        )

    def pick(b):
        total = before[b]
        skip = (total // group) * enc_count + jnp.clip(total % group - enc_count * s, 0, enc_count)
        local = skip + lax.broadcasted_iota(jnp.int32, (window, HD), 0)
        index = (local % enc_count) * vis_rows + local // enc_count
        chosen = one_hot(index.astype(jnp.float32), enc_count * vis_rows)
        table = seen[...].reshape(enc_count * vis_rows, features)
        return jnp.dot(chosen, table, preferred_element_type=jnp.float32).astype(jnp.bfloat16)

    def move(k):
        to = (s + k) % seq_count
        return send(picked.at[to], landed.at[s], blk_s.at[k], blk_r.at[k], to, e)

    @pl.loop(1, seq_count)
    def _(k):
        to = (s + k) % seq_count
        picked[to] = pick(to)
        move(k).start()

    landed[s] = pick(s)

    @pl.loop(1, side)
    def _(k):
        weigh(k).wait_recv()
        pass_weights(k).start()

    @pl.loop(1, seq_count)
    def _(k):
        move(k).wait_recv()

    def at(c):
        return pl.ds(pl.multiple_of(c * CHUNK, CHUNK), CHUNK)

    def half_of(k, c):
        return pl.ds(pl.multiple_of(c * CHUNK + (k // 2) * (CHUNK // 2), CHUNK // 2), CHUNK // 2)

    def share(k, c):
        return send(xall.at[x, at(c)], xall.at[x, at(c)], x_s.at[k, c], x_r.at[k, c], s, across(k))

    def relay(k, c):
        here = xall.at[(x + side - k) % side, half_of(k, c)]
        return send(here, here, xf_s.at[k, c], xf_r.at[k, c], s, across(k))

    def reach(k, c):
        return send(
            psend.at[(z + side // 2) % side, half_of(k, c)], pmid.at[half_of(k, c)],
            pf_s.at[k, c], pf_r.at[k, c], s, along(k),
        )

    def reduce(k, c):
        return send(
            psend.at[(z + k) % side, at(c)], precv.at[k // 2, at(c)],
            p_s.at[k, c], p_r.at[k, c], s, along(k),
        )

    def trade(c):
        return send(qown.at[at(c)], q_out.at[at(c)], q_s.at[c], q_r.at[c], other, e)

    def norms(k, c):
        return send(squares.at[c], sqrecv.at[k, c], n_s.at[k, c], n_r.at[k, c], s, along(k))

    def keys(owner, c):
        return pl.ds(pl.multiple_of(owner * rows + c * CHUNK, CHUNK), CHUNK)

    def pair(c):
        here = kv_out.at[e % 2, keys(s, c)]
        return send(here, here, kx_s.at[c], kx_r.at[c], s, mate)

    def column(k, c):
        here = kv_out.at[:, keys(s, c)]
        return send(here, here, ky_s.at[k, c], ky_r.at[k, c], column_of(k), e)

    def chip(k, c):
        here = kv_out.at[:, keys(column_of(ys - k), c)]
        return send(here, here, kc_s.at[k, c], kc_r.at[k, c], twin, e)

    ones = jnp.ones((8, side * features), jnp.bfloat16)

    def push(c):
        index = spread(slots[pl.ds(c, 1), :])
        chosen = one_hot(index, landed.shape[0] * window)
        table = landed[...].reshape(landed.shape[0] * window, features)
        frame = jnp.dot(chosen, table, preferred_element_type=jnp.float32).astype(jnp.bfloat16)
        visual = jnp.concatenate([index] * (features // HD), axis=1) >= 0
        xall[x, at(c)] = jnp.where(visual, frame, text_ref[at(c), :])
        lim_out[at(c), :] = spread(lims[pl.ds(c, 1), :])
        for k in sides:
            share(k, c).start()

    def hop(c):
        for k in sides:
            share(k, c).wait_recv()
            relay(k, c).start()

    def multiply(c):
        @pl.when(c == 0)
        def _():
            for k in range(1, side):
                pass_weights(k).wait_recv()

        for k in sides:
            relay(k, c).wait_recv()
        block = jnp.concatenate([xall[j, at(c)] for j in range(side)], axis=1)
        wide = block.astype(jnp.float32)
        squares[c] = lax.dot_general(
            ones, (wide * wide).astype(jnp.bfloat16), (((1,), (1,)), ((), ())),
            preferred_element_type=jnp.float32,
        )
        for k in range(1, side):
            norms(k, c).start()
        weights = wall[...].reshape(side * features, side * columns)
        partial = jnp.dot(block, weights, preferred_element_type=jnp.float32).astype(jnp.bfloat16)
        for zz in range(side):
            psend[zz, at(c)] = partial[:, zz * columns : (zz + 1) * columns]
        for k in sides:
            reach(k, c).start()

    def merge(c):
        for k in sides:
            reach(k, c).wait_recv()
            rows_here = half_of(k, c)
            target = (z + k) % side
            joined = psend[target, rows_here].astype(jnp.float32) + pmid[rows_here].astype(jnp.float32)
            psend[target, rows_here] = joined.astype(jnp.bfloat16)
            reduce(k, c).start()

    def finish(c):
        total = psend[z, at(c)].astype(jnp.float32)
        square = squares[c]
        for k in sides:
            reduce(k, c).wait_recv()
            total = total + precv[k // 2, at(c)].astype(jnp.float32)
        for k in range(1, side):
            norms(k, c).wait_recv()
            square = square + sqrecv[k, c]
        scale = spread(lax.rsqrt(square / (features * enc_count) + EPS)[0:1, :])
        factor = math.log2(math.e) / HD**0.5
        for j in range(q_columns // HD):
            lanes = slice(j * HD, (j + 1) * HD)
            qown[at(c), lanes] = (total[:, lanes] * (scale * factor)).astype(jnp.bfloat16)

        @pl.when(c >= chunks // 2)
        def _():
            q_out[at(c), :] = qown[at(c), :]

        @pl.when(c < chunks // 2)
        def _():
            trade(c).start()

        kv_out[e % 2, keys(s, c)] = (total[:, q_columns:] * scale).astype(jnp.bfloat16)
        pair(c).start()

    def spread_out(c):
        pair(c).wait_recv()
        for k in range(1, ys):
            column(k, c).start()
        chip(0, c).start()

    def hand_over(c):
        for k in range(1, ys):
            column(k, c).wait_recv()
            chip(k, c).start()

    stages = (push, hop, multiply, merge, finish, spread_out, hand_over)
    lags = (0, 2, 3, 4, 5, 6, 8)

    @pl.loop(0, chunks + lags[-1])
    def _(t):
        for stage, lag in zip(stages, lags):
            @pl.when((t >= lag) & (t < chunks + lag))
            def _():
                stage(t - lag)

    @pl.loop(0, chunks)
    def _(c):
        pair(c).wait_send()
        chip(0, c).wait()
        for k in range(1, ys):
            chip(k, c).wait()
            column(k, c).wait_send()
        for k in sides:
            share(k, c).wait_send()
            relay(k, c).wait_send()
            reach(k, c).wait_send()
            reduce(k, c).wait_send()
        for k in range(1, side):
            norms(k, c).wait_send()

    @pl.loop(0, chunks // 2)
    def _(c):
        trade(c).wait()

    @pl.loop(1, side)
    def _(k):
        weigh(k).wait_send()
        pass_weights(k).wait_send()

    @pl.loop(1, enc_count)
    def _(k):
        see(k).wait_send()

    @pl.loop(1, seq_count)
    def _(k):
        move(k).wait_send()


def project(text, visual, gain, w_query, w_keyval, image_count, text_gap):
    rows, features = text.shape
    vis_rows = pl.cdiv(visual.shape[0], 16) * 16
    seq_count, enc_count = lax.axis_size("seq"), lax.axis_size("enc")
    side, ys = math.isqrt(enc_count), seq_count // 2
    q_columns = w_query.shape[1] // enc_count
    columns = q_columns + w_keyval.shape[1] // enc_count
    chunks = rows // CHUNK
    window = rows // seq_count
    bf16, f32 = jnp.bfloat16, jnp.float32

    def dma(*shape):
        return [pltpu.SemaphoreType.DMA(shape)] * 2

    return pl.pallas_call(
        functools.partial(project_kernel, side),
        out_shape=(
            jax.ShapeDtypeStruct((rows, q_columns), bf16),
            jax.ShapeDtypeStruct((2, rows * seq_count, HD), bf16),
            jax.ShapeDtypeStruct((rows, HD), f32),
        ),
        in_specs=[pl.BlockSpec(memory_space=pltpu.SMEM)] * 2
        + [pl.BlockSpec(memory_space=VMEM), pl.BlockSpec(memory_space=pl.ANY)]
        + [pl.BlockSpec(memory_space=VMEM)] * 3,
        out_specs=tuple([pl.BlockSpec(memory_space=VMEM)] * 3),
        scratch_shapes=[
            pltpu.SMEM((seq_count,), jnp.int32),
            VMEM((side, features, side * columns), bf16),
            VMEM((side, features, side * columns), bf16),
            VMEM((enc_count, vis_rows, features), bf16),
            VMEM((seq_count, window, features), bf16),
            VMEM((seq_count, window, features), bf16),
            VMEM((16, HD), f32),
            VMEM((16, HD), f32),
            VMEM((side, rows, features), bf16),
            VMEM((side, rows, columns), bf16),
            VMEM((rows, columns), bf16),
            VMEM((2, rows, columns), bf16),
            VMEM((chunks, 8, CHUNK), f32),
            VMEM((side, chunks, 8, CHUNK), f32),
            VMEM((rows, q_columns), bf16),
            *dma(enc_count),
            *dma(seq_count),
            *dma(side),
            *dma(side),
            *dma(side, chunks),
            *dma(side, chunks),
            *dma(side, chunks),
            *dma(side, chunks),
            *dma(side, chunks),
            *dma(chunks),
            *dma(ys, chunks),
            *dma(ys, chunks),
            *dma(chunks),
        ],
        compiler_params=pltpu.CompilerParams(
            collective_id=0, has_side_effects=True, vmem_limit_bytes=60 << 20
        ),
    )(image_count, text_gap, text, visual, gain, w_query, w_keyval)


def attention_kernel(bq, bk, sbq, sbk, off_ref, q_ref, kv_ref, lim_ref, o_ref, acc, den, top):
    heads = q_ref.shape[1] // HD
    rows_all, keys_all = q_ref.shape[0], kv_ref.shape[1]
    q0 = off_ref[0]

    def query_norm(step, best):
        block = q_ref[pl.ds(pl.multiple_of(step * 128, 128), 128), :].astype(jnp.float32)
        square = block * block
        for head in range(heads):
            norm = jnp.sum(square[:, head * HD : (head + 1) * HD], axis=1, keepdims=True)
            best = jnp.maximum(best, norm)
        return best

    ones = jnp.ones((HD, HD), jnp.bfloat16)

    def key_norm(step, best):
        block = kv_ref[0, pl.ds(pl.multiple_of(step * bk, bk), bk), :]
        norm = jnp.dot(block * block, ones, preferred_element_type=jnp.float32)
        return jnp.maximum(best, jnp.max(norm.reshape(bk // 8, 8, HD), axis=0))

    zero = jnp.zeros((128, 1), jnp.float32)
    largest_query = jnp.max(lax.fori_loop(0, rows_all // 128, query_norm, zero))
    largest_key = jnp.max(lax.fori_loop(0, keys_all // bk, key_norm, jnp.zeros((8, HD), jnp.float32)))
    safe = largest_query * largest_key * 1.02 < SAFE * SAFE

    def scores(row, head, size, key, count, masked):
        q = q_ref[pl.ds(row, size), head * HD : (head + 1) * HD]
        s = lax.dot_general(
            q,
            kv_ref[0, pl.ds(key, count), :],
            (((1,), (1,)), ((), ())),
            preferred_element_type=jnp.float32,
        )
        if masked:
            at = (key + lax.broadcasted_iota(jnp.int32, (size, count), 1)).astype(jnp.float32)
            lim = jnp.concatenate([lim_ref[pl.ds(row, size), :]] * (count // HD), axis=1)
            s = jnp.where(at <= lim, s, NEG)
        return s

    def lane_sums(p):
        total = p[:, :HD]
        for part in range(1, p.shape[1] // HD):
            total = total + p[:, part * HD : (part + 1) * HD]
        return total

    def tiles(size, count, begin, step, end):
        @pl.loop(0, rows_all // size)
        def _(tile):
            row = pl.multiple_of(tile * size, size)
            begin()
            first = q0 + row
            whole = first // count
            last = jnp.minimum(pl.cdiv(first + size + 255, count), keys_all // count)

            @pl.loop(0, whole)
            def _(j):
                step(row, pl.multiple_of(j * count, count), False)

            @pl.loop(whole, last)
            def _(j):
                step(row, pl.multiple_of(j * count, count), True)

            end(row)

    @pl.when(safe)
    def _():
        def begin():
            acc[...] = jnp.zeros_like(acc)
            den[...] = jnp.zeros_like(den)

        def step(row, key, masked):
            values = kv_ref[1, pl.ds(key, bk), :]
            for head in range(heads):
                p = jnp.exp2(scores(row, head, bq, key, bk, masked))
                acc[head] += jnp.dot(
                    p.astype(jnp.bfloat16), values, preferred_element_type=jnp.float32
                )
                den[head] += lane_sums(p)

        def end(row):
            for head in range(heads):
                result = acc[head] / jnp.sum(den[head], axis=1, keepdims=True)
                o_ref[pl.ds(row, bq), head * HD : (head + 1) * HD] = result.astype(jnp.bfloat16)

        tiles(bq, bk, begin, step, end)

    @pl.when(jnp.logical_not(safe))
    def _():
        part = pl.ds(0, sbq)

        def begin():
            acc[...] = jnp.zeros_like(acc)
            den[...] = jnp.zeros_like(den)
            top[...] = jnp.full_like(top, NEG)

        def step(row, key, masked):
            values = kv_ref[1, pl.ds(key, sbk), :]
            for head in range(heads):
                s = scores(row, head, sbq, key, sbk, masked)
                old = top[head]
                new = jnp.maximum(old, jnp.max(s, axis=1, keepdims=True))
                top[head] = new
                p = jnp.exp2(s - new)
                shrink = jnp.exp2(old - new)
                acc[head, part] = acc[head, part] * shrink + jnp.dot(
                    p.astype(jnp.bfloat16), values, preferred_element_type=jnp.float32
                )
                den[head, part] = den[head, part] * shrink + lane_sums(p)

        def end(row):
            for head in range(heads):
                result = acc[head, part] / jnp.sum(den[head, part], axis=1, keepdims=True)
                o_ref[pl.ds(row, sbq), head * HD : (head + 1) * HD] = result.astype(jnp.bfloat16)

        tiles(sbq, sbk, begin, step, end)


def attention(q0, query, keyval, lim, part):
    rows, width = query.shape[0] // 2, query.shape[1]
    heads = width // HD
    bq, bk, sbq, sbk = rows, 1024, 128, 512
    flops = 4 * rows * keyval.shape[1] * width
    return pl.pallas_call(
        functools.partial(attention_kernel, bq, bk, sbq, sbk),
        out_shape=jax.ShapeDtypeStruct((rows, width), jnp.bfloat16),
        grid=(1,),
        in_specs=[
            pl.BlockSpec(memory_space=pltpu.SMEM),
            pl.BlockSpec((rows, width), lambda i: (part, 0)),
            pl.BlockSpec(memory_space=VMEM),
            pl.BlockSpec((rows, HD), lambda i: (part, 0)),
        ],
        out_specs=pl.BlockSpec(memory_space=VMEM),
        scratch_shapes=[
            VMEM((heads, bq, HD), jnp.float32),
            VMEM((heads, bq, HD), jnp.float32),
            VMEM((heads, sbq, 1), jnp.float32),
        ],
        compiler_params=pltpu.CompilerParams(vmem_limit_bytes=56 << 20),
        cost_estimate=pl.CostEstimate(
            flops=flops, bytes_accessed=keyval.size * 2, transcendentals=rows * keyval.shape[1]
        ),
    )(q0, query, keyval, lim)


def per_device(text, visual, gain, w_query, w_keyval, image_count, text_gap):
    rows = text.shape[0]
    query, keyval, lim = project(
        text, visual, gain, w_query, w_keyval, image_count, text_gap
    )
    half = rows // 2
    seq_count = lax.axis_size("seq")
    mine = (lax.axis_index("seq") * rows).astype(jnp.int32)
    theirs = (seq_count - 1) * rows - mine
    lent = attention(theirs.reshape(1), query, keyval, lim, 0)
    back = lax.ppermute(lent, "seq", [(i, seq_count - 1 - i) for i in range(seq_count)])
    own = attention((mine + half).reshape(1), query, keyval, lim, 1)
    return jnp.concatenate((back, own), axis=0)


def solution(mesh):
    in_specs = (
        P("seq", "enc"),
        P(("seq", "enc"), None),
        P("enc"),
        P("enc", None),
        P("enc", None),
        P(),
        P(),
    )
    out_specs = P("seq", "enc")
    return jax.shard_map(
        per_device, mesh=mesh, in_specs=in_specs, out_specs=out_specs, check_vma=False
    )
```

```python
import functools
import math

import jax
import jax.numpy as jnp
from jax import lax
from jax.experimental import pallas as pl
from jax.experimental.pallas import tpu as pltpu
from jax.sharding import PartitionSpec as P

HD = 128
EPS = 1e-05
CHUNK = 128
MESH = pl.DeviceIdType.MESH
NEG = -1e30
SAFE = 64.0
VMEM = pltpu.VMEM


def spread(row):
    return jnp.broadcast_to(row, (HD, HD)).T


def project_kernel(
    side, count_ref, gap_ref, text_ref, visual_ref, gain_ref, wq_ref, wkv_ref,
    q_out, kv_out, lim_out, safe_out,
    before, wsend, wall, seen, picked, landed, slots, lims, xall, psend, pmid, precv, squares,
    sqrecv, qown, peak, peaks,
    vis_s, vis_r, blk_s, blk_r, w_s, w_r, wf_s, wf_r, x_s, x_r, xf_s, xf_r, p_s, p_r, pf_s, pf_r,
    n_s, n_r, kx_s, kx_r, ky_s, ky_r, kc_s, kc_r, q_s, q_r, m_s, m_r,
):
    seq_count, enc_count = lax.axis_size("seq"), lax.axis_size("enc")
    s, e = lax.axis_index("seq"), lax.axis_index("enc")
    y, core, z, x = s // 2, s % 2, e // side, e % side
    ys = seq_count // 2
    rows, features = text_ref.shape
    chunks = rows // CHUNK
    window = landed.shape[1]
    vis_rows = seen.shape[1]
    columns = psend.shape[2]
    q_columns = q_out.shape[1]
    k_columns = columns - q_columns
    half = wall.shape[2] // 2
    images = count_ref.shape[0]
    twin = s + 1 - 2 * core
    mate = e + 1 - 2 * (e % 2)
    other = seq_count - 1 - s
    sides = (1, side - 1)

    def across(k):
        return z * side + (x + k) % side

    def along(k):
        return ((z + k) % side) * side + x

    def column_of(k):
        return ((y + k) % ys) * 2 + core

    def send(source, target, ssem, rsem, to_s, to_e):
        return pltpu.make_async_remote_copy(
            src_ref=source, dst_ref=target, send_sem=ssem, recv_sem=rsem,
            device_id=(to_s, to_e), device_id_type=MESH,
        )

    seen[...] = jnp.zeros_like(seen)
    barrier = pltpu.get_barrier_semaphore()

    @pl.loop(1, enc_count)
    def _(k):
        pl.semaphore_signal(barrier, inc=1, device_id=(s, (e + k) % enc_count), device_id_type=MESH)

    @pl.loop(1, seq_count)
    def _(k):
        pl.semaphore_signal(barrier, inc=1, device_id=((s + k) % seq_count, e), device_id_type=MESH)

    pl.semaphore_wait(barrier, enc_count + seq_count - 2)

    def see(k):
        to = (e + k) % enc_count
        lanes = pl.ds(pl.multiple_of(to * features, features), features)
        there = seen.at[e, pl.ds(0, visual_ref.shape[0])]
        return send(visual_ref.at[:, lanes], there, vis_s.at[k], vis_r.at[k], s, to)

    @pl.loop(1, enc_count)
    def _(k):
        see(k).start()

    kept = pltpu.make_async_copy(
        visual_ref.at[:, pl.ds(pl.multiple_of(e * features, features), features)],
        seen.at[e, pl.ds(0, visual_ref.shape[0])],
        vis_s.at[0],
    )
    kept.start()

    gains = [
        spread(gain_ref[g * HD : (g + 1) * HD].astype(jnp.float32).reshape(1, HD)) for g in range(features // HD)
    ]

    def scaled(ref, part, start):
        lanes = pl.ds(pl.multiple_of(start, HD), HD)
        block = ref[part * HD : (part + 1) * HD, lanes].astype(jnp.float32)
        return (block * gains[part]).astype(jnp.bfloat16)

    @pl.loop(0, side)
    def _(to):
        for zz in range(side):
            for part in range(features // HD):
                there = pl.ds(part * HD, HD)
                owner = zz * side + to
                for j in range(q_columns // HD):
                    wsend[to, there, pl.ds(zz * columns + j * HD, HD)] = scaled(
                        wq_ref, part, owner * q_columns + j * HD
                    )
                for j in range(k_columns // HD):
                    wsend[to, there, pl.ds(zz * columns + q_columns + j * HD, HD)] = scaled(
                        wkv_ref, part, owner * k_columns + j * HD
                    )

    mine = pl.ds(pl.multiple_of(core * half, HD), half)

    def weigh(k):
        return send(
            wsend.at[(x + k) % side, :, mine], wall.at[x, :, mine],
            w_s.at[k], w_r.at[k], s, across(k),
        )

    def pass_weights(k):
        origin = (x + side - k) % side
        return send(
            wall.at[origin, :, mine], wall.at[origin, :, mine], wf_s.at[k], wf_r.at[k], twin, e
        )

    @pl.loop(1, side)
    def _(k):
        weigh(k).start()

    wall[x] = wsend[x]

    shape = slots.shape
    position = (
        s * rows
        + lax.broadcasted_iota(jnp.int32, shape, 0) * CHUNK
        + lax.broadcasted_iota(jnp.int32, shape, 1)
    )

    seat = jnp.where(
        lax.broadcasted_iota(jnp.int32, shape, 0) >= chunks // 2, position, position + (other - s) * rows
    )

    def place(i, carry):
        end, offset, shift, lim, counts = carry
        start = end + gap_ref[i]
        count = count_ref[i]
        end = start + count
        inside = (position >= start) & (position < end)
        shift = jnp.where(inside, offset - start, shift)
        lim = jnp.where((seat >= start) & (seat < end), end - 1, lim)
        counts = tuple(
            total + jnp.minimum(jnp.maximum(b * rows - start, 0), count)
            for b, total in enumerate(counts)
        )
        return end, offset + count, shift, lim, counts

    none = jnp.full(shape, 1, jnp.int32)
    zero = jnp.int32(0)
    _, _, shift, lim, counts = lax.fori_loop(
        0, images, place, (zero, zero, none, seat, (zero,) * seq_count)
    )
    for b in range(seq_count):
        before[b] = counts[b]
    lims[...] = lim.astype(jnp.float32)
    token = position + shift
    origin = (token // enc_count) % seq_count
    total = before[s]
    group = seq_count * enc_count
    skipped = (total // group) * enc_count + jnp.clip(total % group - enc_count * origin, 0, enc_count)
    slot = origin * window + (token // group) * enc_count + token % enc_count - skipped
    slots[...] = jnp.where(shift <= 0, slot, -1).astype(jnp.float32)

    @pl.loop(1, enc_count)
    def _(k):
        see(k).wait_recv()

    kept.wait()

    def one_hot(index, count):
        lane = lax.broadcasted_iota(jnp.int32, index.shape, 1).astype(jnp.float32)
        return jnp.concatenate(
            [jnp.where(index == lane + j * HD, 1.0, 0.0).astype(jnp.bfloat16) for j in range(count // HD)],
            axis=1,
        )

    def pick(b):
        total = before[b]
        skip = (total // group) * enc_count + jnp.clip(total % group - enc_count * s, 0, enc_count)
        local = skip + lax.broadcasted_iota(jnp.int32, (window, HD), 0)
        index = (local % enc_count) * vis_rows + local // enc_count
        chosen = one_hot(index.astype(jnp.float32), enc_count * vis_rows)
        table = seen[...].reshape(enc_count * vis_rows, features)
        return jnp.dot(chosen, table, preferred_element_type=jnp.float32).astype(jnp.bfloat16)

    def move(k):
        to = (s + k) % seq_count
        return send(picked.at[to], landed.at[s], blk_s.at[k], blk_r.at[k], to, e)

    @pl.loop(1, seq_count)
    def _(k):
        to = (s + k) % seq_count
        picked[to] = pick(to)
        move(k).start()

    landed[s] = pick(s)

    @pl.loop(1, side)
    def _(k):
        weigh(k).wait_recv()
        pass_weights(k).start()

    @pl.loop(1, seq_count)
    def _(k):
        move(k).wait_recv()

    def at(c):
        return pl.ds(pl.multiple_of(c * CHUNK, CHUNK), CHUNK)

    def half_of(k, c):
        return pl.ds(pl.multiple_of(c * CHUNK + (k // 2) * (CHUNK // 2), CHUNK // 2), CHUNK // 2)

    def share(k, c):
        return send(xall.at[x, at(c)], xall.at[x, at(c)], x_s.at[k, c], x_r.at[k, c], s, across(k))

    def relay(k, c):
        here = xall.at[(x + side - k) % side, half_of(k, c)]
        return send(here, here, xf_s.at[k, c], xf_r.at[k, c], s, across(k))

    def reach(k, c):
        return send(
            psend.at[(z + side // 2) % side, half_of(k, c)], pmid.at[half_of(k, c)],
            pf_s.at[k, c], pf_r.at[k, c], s, along(k),
        )

    def reduce(k, c):
        return send(
            psend.at[(z + k) % side, at(c)], precv.at[k // 2, at(c)],
            p_s.at[k, c], p_r.at[k, c], s, along(k),
        )

    def trade(c):
        return send(qown.at[at(c)], q_out.at[at(c)], q_s.at[c], q_r.at[c], other, e)

    def norms(k, c):
        return send(squares.at[c], sqrecv.at[k, c], n_s.at[k, c], n_r.at[k, c], s, along(k))

    def keys(owner, c):
        return pl.ds(pl.multiple_of(owner * rows + c * CHUNK, CHUNK), CHUNK)

    def pair(c):
        here = kv_out.at[e % 2, keys(s, c)]
        return send(here, here, kx_s.at[c], kx_r.at[c], s, mate)

    def column(k, c):
        here = kv_out.at[:, keys(s, c)]
        return send(here, here, ky_s.at[k, c], ky_r.at[k, c], column_of(k), e)

    def chip(k, c):
        here = kv_out.at[:, keys(column_of(ys - k), c)]
        return send(here, here, kc_s.at[k, c], kc_r.at[k, c], twin, e)

    ones = jnp.ones((8, side * features), jnp.bfloat16)

    def push(c):
        index = spread(slots[pl.ds(c, 1), :])
        chosen = one_hot(index, landed.shape[0] * window)
        table = landed[...].reshape(landed.shape[0] * window, features)
        frame = jnp.dot(chosen, table, preferred_element_type=jnp.float32).astype(jnp.bfloat16)
        visual = jnp.concatenate([index] * (features // HD), axis=1) >= 0
        xall[x, at(c)] = jnp.where(visual, frame, text_ref[at(c), :])
        lim_out[at(c), :] = spread(lims[pl.ds(c, 1), :])
        for k in sides:
            share(k, c).start()

    def hop(c):
        for k in sides:
            share(k, c).wait_recv()
            relay(k, c).start()

    def multiply(c):
        @pl.when(c == 0)
        def _():
            for k in range(1, side):
                pass_weights(k).wait_recv()

        for k in sides:
            relay(k, c).wait_recv()
        block = jnp.concatenate([xall[j, at(c)] for j in range(side)], axis=1)
        wide = block.astype(jnp.float32)
        squares[c] = lax.dot_general(
            ones, (wide * wide).astype(jnp.bfloat16), (((1,), (1,)), ((), ())),
            preferred_element_type=jnp.float32,
        )
        for k in range(1, side):
            norms(k, c).start()
        weights = wall[...].reshape(side * features, side * columns)
        partial = jnp.dot(block, weights, preferred_element_type=jnp.float32).astype(jnp.bfloat16)
        for zz in range(side):
            psend[zz, at(c)] = partial[:, zz * columns : (zz + 1) * columns]
        for k in sides:
            reach(k, c).start()

    def merge(c):
        for k in sides:
            reach(k, c).wait_recv()
            rows_here = half_of(k, c)
            target = (z + k) % side
            joined = psend[target, rows_here].astype(jnp.float32) + pmid[rows_here].astype(jnp.float32)
            psend[target, rows_here] = joined.astype(jnp.bfloat16)
            reduce(k, c).start()

    def finish(c):
        total = psend[z, at(c)].astype(jnp.float32)
        square = squares[c]
        for k in sides:
            reduce(k, c).wait_recv()
            total = total + precv[k // 2, at(c)].astype(jnp.float32)
        for k in range(1, side):
            norms(k, c).wait_recv()
            square = square + sqrecv[k, c]
        scale = spread(lax.rsqrt(square / (features * enc_count) + EPS)[0:1, :])
        factor = math.log2(math.e) / HD**0.5
        query_norm = jnp.zeros((CHUNK, 1), jnp.float32)
        for j in range(q_columns // HD):
            lanes = slice(j * HD, (j + 1) * HD)
            asked = (total[:, lanes] * (scale * factor)).astype(jnp.bfloat16)
            qown[at(c), lanes] = asked
            asked = asked.astype(jnp.float32)
            query_norm = jnp.maximum(query_norm, jnp.sum(asked * asked, axis=1, keepdims=True))

        @pl.when(c >= chunks // 2)
        def _():
            q_out[at(c), :] = qown[at(c), :]

        @pl.when(c < chunks // 2)
        def _():
            trade(c).start()

        held = (total[:, q_columns:] * scale).astype(jnp.bfloat16)
        kv_out[e % 2, keys(s, c)] = held
        pair(c).start()
        held = held.astype(jnp.float32)
        key_norm = jnp.sum(held * held, axis=1, keepdims=True) * (1 - e % 2).astype(jnp.float32)
        for i, norm in enumerate((query_norm, key_norm)):
            wide = jnp.broadcast_to(norm, (CHUNK, HD)).reshape(CHUNK // 8, 8, HD)
            peak[0, i] = jnp.maximum(peak[0, i], jnp.max(wide, axis=0))

    def meet(step, k):
        goal = ((s, across(k)), (s, along(k)), ((s + k) % seq_count, e))[step]
        return send(
            peak.at[step], peaks.at[step, k], m_s.at[step, k], m_r.at[step, k], goal[0], goal[1]
        )

    sizes = (side, side, seq_count)

    def climb(step, c):
        @pl.when(c == chunks - 1)
        def _():
            if step > 0:
                highest = peak[step - 1]
                for k in range(1, sizes[step - 1]):
                    meet(step - 1, k).wait_recv()
                    highest = jnp.maximum(highest, peaks[step - 1, k])
                if step < len(sizes):
                    peak[step] = highest
                else:
                    bound = jnp.max(highest[0]) * jnp.max(highest[1])
                    safe_out[0] = jnp.where(bound < SAFE * SAFE, 1, 0).astype(jnp.int32)
            if step < len(sizes):
                for k in range(1, sizes[step]):
                    meet(step, k).start()

    def spread_out(c):
        pair(c).wait_recv()
        for k in range(1, ys):
            column(k, c).start()
        chip(0, c).start()

    def hand_over(c):
        for k in range(1, ys):
            column(k, c).wait_recv()
            chip(k, c).start()

    climbs = [functools.partial(climb, step) for step in range(len(sizes) + 1)]
    stages = (
        push, hop, multiply, merge, finish, climbs[0], spread_out, climbs[1], climbs[2],
        hand_over, climbs[3],
    )
    lags = (0, 2, 3, 4, 5, 5, 6, 6, 7, 8, 8)
    peak[...] = jnp.zeros_like(peak)

    @pl.loop(0, chunks + lags[-1])
    def _(t):
        for stage, lag in zip(stages, lags):
            @pl.when((t >= lag) & (t < chunks + lag))
            def _():
                stage(t - lag)

    @pl.loop(0, chunks)
    def _(c):
        pair(c).wait_send()
        chip(0, c).wait()
        for k in range(1, ys):
            chip(k, c).wait()
            column(k, c).wait_send()
        for k in sides:
            share(k, c).wait_send()
            relay(k, c).wait_send()
            reach(k, c).wait_send()
            reduce(k, c).wait_send()
        for k in range(1, side):
            norms(k, c).wait_send()

    @pl.loop(0, chunks // 2)
    def _(c):
        trade(c).wait()

    for step, size in enumerate(sizes):
        for k in range(1, size):
            meet(step, k).wait_send()

    @pl.loop(1, side)
    def _(k):
        weigh(k).wait_send()
        pass_weights(k).wait_send()

    @pl.loop(1, enc_count)
    def _(k):
        see(k).wait_send()

    @pl.loop(1, seq_count)
    def _(k):
        move(k).wait_send()


def project(text, visual, gain, w_query, w_keyval, image_count, text_gap):
    rows, features = text.shape
    vis_rows = pl.cdiv(visual.shape[0], 16) * 16
    seq_count, enc_count = lax.axis_size("seq"), lax.axis_size("enc")
    side, ys = math.isqrt(enc_count), seq_count // 2
    q_columns = w_query.shape[1] // enc_count
    columns = q_columns + w_keyval.shape[1] // enc_count
    chunks = rows // CHUNK
    window = rows // seq_count
    bf16, f32 = jnp.bfloat16, jnp.float32

    def dma(*shape):
        return [pltpu.SemaphoreType.DMA(shape)] * 2

    return pl.pallas_call(
        functools.partial(project_kernel, side),
        out_shape=(
            jax.ShapeDtypeStruct((rows, q_columns), bf16),
            jax.ShapeDtypeStruct((2, rows * seq_count, HD), bf16),
            jax.ShapeDtypeStruct((rows, HD), f32),
            jax.ShapeDtypeStruct((1,), jnp.int32),
        ),
        in_specs=[pl.BlockSpec(memory_space=pltpu.SMEM)] * 2
        + [pl.BlockSpec(memory_space=VMEM), pl.BlockSpec(memory_space=pl.ANY)]
        + [pl.BlockSpec(memory_space=VMEM)] * 3,
        out_specs=tuple(
            [pl.BlockSpec(memory_space=VMEM)] * 3 + [pl.BlockSpec(memory_space=pltpu.SMEM)]
        ),
        scratch_shapes=[
            pltpu.SMEM((seq_count,), jnp.int32),
            VMEM((side, features, side * columns), bf16),
            VMEM((side, features, side * columns), bf16),
            VMEM((enc_count, vis_rows, features), bf16),
            VMEM((seq_count, window, features), bf16),
            VMEM((seq_count, window, features), bf16),
            VMEM((16, HD), f32),
            VMEM((16, HD), f32),
            VMEM((side, rows, features), bf16),
            VMEM((side, rows, columns), bf16),
            VMEM((rows, columns), bf16),
            VMEM((2, rows, columns), bf16),
            VMEM((chunks, 8, CHUNK), f32),
            VMEM((side, chunks, 8, CHUNK), f32),
            VMEM((rows, q_columns), bf16),
            VMEM((3, 2, 8, HD), f32),
            VMEM((3, seq_count, 2, 8, HD), f32),
            *dma(enc_count),
            *dma(seq_count),
            *dma(side),
            *dma(side),
            *dma(side, chunks),
            *dma(side, chunks),
            *dma(side, chunks),
            *dma(side, chunks),
            *dma(side, chunks),
            *dma(chunks),
            *dma(ys, chunks),
            *dma(ys, chunks),
            *dma(chunks),
            *dma(3, seq_count),
        ],
        compiler_params=pltpu.CompilerParams(
            collective_id=0, has_side_effects=True, vmem_limit_bytes=60 << 20
        ),
    )(image_count, text_gap, text, visual, gain, w_query, w_keyval)


def masked_scores(q, keys, lim, key):
    s = lax.dot_general(q, keys, (((1,), (1,)), ((), ())), preferred_element_type=jnp.float32)
    if lim is None:
        return s
    at = (key + lax.broadcasted_iota(jnp.int32, s.shape, 1)).astype(jnp.float32)
    return jnp.where(at <= jnp.concatenate([lim] * (s.shape[1] // HD), axis=1), s, NEG)


def lane_sums(p):
    total = p[:, :HD]
    for part in range(1, p.shape[1] // HD):
        total = total + p[:, part * HD : (part + 1) * HD]
    return total


def quick_kernel(bk, q_ref, kv_ref, lim_ref, o_ref, kv, lent, acc, den, kv_s, o_s, o_r):
    s, e = lax.axis_index("seq"), lax.axis_index("enc")
    seq_count = lax.axis_size("seq")
    other = seq_count - 1 - s
    heads = q_ref.shape[1] // HD
    rows = q_ref.shape[0]
    half = rows // 2
    blocks = kv_ref.shape[1] // bk

    def load(j):
        here = pl.ds(pl.multiple_of(j * bk, bk), bk)
        return pltpu.make_async_copy(kv_ref.at[:, here], kv.at[:, here], kv_s.at[j])

    @pl.loop(0, blocks)
    def _(j):
        load(j).start()

    barrier = pltpu.get_barrier_semaphore()
    pl.semaphore_signal(barrier, inc=1, device_id=(other, e), device_id_type=MESH)

    def job(part, first, ready, target, base):
        size = half
        rows_here = pl.ds(part * half, half)
        acc[...] = jnp.zeros_like(acc)
        den[...] = jnp.zeros_like(den)
        whole = first // bk
        last = jnp.minimum((first + size + 255 + bk - 1) // bk, blocks)

        def step(j, masked):
            @pl.when(j >= ready)
            def _():
                load(j).wait()

            key = pl.multiple_of(j * bk, bk)
            keys, values = kv[0, pl.ds(key, bk), :], kv[1, pl.ds(key, bk), :]
            lim = lim_ref[rows_here, :] if masked else None
            for head in range(heads):
                q = q_ref[rows_here, head * HD : (head + 1) * HD]
                p = jnp.exp2(masked_scores(q, keys, lim, key))
                acc[head] += jnp.dot(
                    p.astype(jnp.bfloat16), values, preferred_element_type=jnp.float32
                )
                den[head] += lane_sums(p)

        @pl.loop(0, whole)
        def _(j):
            step(j, False)

        @pl.loop(whole, last)
        def _(j):
            step(j, True)

        for head in range(heads):
            result = acc[head] / jnp.sum(den[head], axis=1, keepdims=True)
            target[base : base + half, head * HD : (head + 1) * HD] = result.astype(jnp.bfloat16)
        return last

    used = job(0, other * rows, 0, lent, 0)
    pl.semaphore_wait(barrier, 1)
    back = pltpu.make_async_remote_copy(
        src_ref=lent, dst_ref=o_ref.at[pl.ds(0, half)], send_sem=o_s, recv_sem=o_r,
        device_id=(other, e), device_id_type=MESH,
    )
    back.start()
    used = jnp.maximum(used, job(1, s * rows + half, used, o_ref, half))

    @pl.loop(used, blocks)
    def _(j):
        load(j).wait()

    back.wait()


def quick(query, keyval, lim):
    rows, width = query.shape
    heads, bk = width // HD, 1024
    return pl.pallas_call(
        functools.partial(quick_kernel, bk),
        out_shape=jax.ShapeDtypeStruct((rows, width), jnp.bfloat16),
        in_specs=[
            pl.BlockSpec(memory_space=VMEM),
            pl.BlockSpec(memory_space=pl.ANY),
            pl.BlockSpec(memory_space=VMEM),
        ],
        out_specs=pl.BlockSpec(memory_space=VMEM),
        scratch_shapes=[
            VMEM(keyval.shape, jnp.bfloat16),
            VMEM((rows // 2, width), jnp.bfloat16),
            VMEM((heads, rows // 2, HD), jnp.float32),
            VMEM((heads, rows // 2, HD), jnp.float32),
            pltpu.SemaphoreType.DMA((keyval.shape[1] // bk,)),
            pltpu.SemaphoreType.DMA,
            pltpu.SemaphoreType.DMA,
        ],
        compiler_params=pltpu.CompilerParams(
            collective_id=1, has_side_effects=True, vmem_limit_bytes=56 << 20
        ),
    )(query, keyval, lim)


def careful_kernel(bq, bk, off_ref, q_ref, kv_ref, lim_ref, o_ref, acc, den, top):
    heads = q_ref.shape[1] // HD

    @pl.loop(0, q_ref.shape[0] // bq)
    def _(tile):
        row = pl.multiple_of(tile * bq, bq)
        acc[...] = jnp.zeros_like(acc)
        den[...] = jnp.zeros_like(den)
        top[...] = jnp.full_like(top, NEG)
        last = jnp.minimum(pl.cdiv(off_ref[0] + row + bq + 255, bk), kv_ref.shape[1] // bk)

        @pl.loop(0, last)
        def _(j):
            key = pl.multiple_of(j * bk, bk)
            keys, values = kv_ref[0, pl.ds(key, bk), :], kv_ref[1, pl.ds(key, bk), :]
            for head in range(heads):
                q = q_ref[pl.ds(row, bq), head * HD : (head + 1) * HD]
                s = masked_scores(q, keys, lim_ref[pl.ds(row, bq), :], key)
                old = top[head]
                new = jnp.maximum(old, jnp.max(s, axis=1, keepdims=True))
                top[head] = new
                p = jnp.exp2(s - new)
                shrink = jnp.exp2(old - new)
                acc[head] = acc[head] * shrink + jnp.dot(
                    p.astype(jnp.bfloat16), values, preferred_element_type=jnp.float32
                )
                den[head] = den[head] * shrink + lane_sums(p)

        for head in range(heads):
            result = acc[head] / jnp.sum(den[head], axis=1, keepdims=True)
            o_ref[pl.ds(row, bq), head * HD : (head + 1) * HD] = result.astype(jnp.bfloat16)


def careful(query, keyval, lim):
    rows, width = query.shape
    half, heads, bq, bk = rows // 2, width // HD, 128, 512
    seq_count = lax.axis_size("seq")
    mine = (lax.axis_index("seq") * rows).astype(jnp.int32)
    theirs = (seq_count - 1) * rows - mine

    def attend(q0, part):
        return pl.pallas_call(
            functools.partial(careful_kernel, bq, bk),
            out_shape=jax.ShapeDtypeStruct((half, width), jnp.bfloat16),
            grid=(1,),
            in_specs=[
                pl.BlockSpec(memory_space=pltpu.SMEM),
                pl.BlockSpec((half, width), lambda i: (part, 0)),
                pl.BlockSpec(memory_space=VMEM),
                pl.BlockSpec((half, HD), lambda i: (part, 0)),
            ],
            out_specs=pl.BlockSpec(memory_space=VMEM),
            scratch_shapes=[
                VMEM((heads, bq, HD), jnp.float32),
                VMEM((heads, bq, HD), jnp.float32),
                VMEM((heads, bq, 1), jnp.float32),
            ],
            compiler_params=pltpu.CompilerParams(vmem_limit_bytes=56 << 20),
        )(q0.reshape(1), query, keyval, lim)

    lent = attend(theirs, 0)
    back = lax.ppermute(lent, "seq", [(i, seq_count - 1 - i) for i in range(seq_count)])
    return jnp.concatenate((back, attend(mine + half, 1)), axis=0)


def per_device(text, visual, gain, w_query, w_keyval, image_count, text_gap):
    query, keyval, lim, safe = project(
        text, visual, gain, w_query, w_keyval, image_count, text_gap
    )
    return lax.cond(safe[0] > 0, quick, careful, query, keyval, lim)


def solution(mesh):
    in_specs = (
        P("seq", "enc"),
        P(("seq", "enc"), None),
        P("enc"),
        P("enc", None),
        P("enc", None),
        P(),
        P(),
    )
    out_specs = P("seq", "enc")
    return jax.shard_map(
        per_device, mesh=mesh, in_specs=in_specs, out_specs=out_specs, check_vma=False
    )
```

```python
import functools
import math

import jax
import jax.numpy as jnp
from jax import lax
from jax.experimental import pallas as pl
from jax.experimental.pallas import tpu as pltpu
from jax.sharding import PartitionSpec as P

HD = 128
EPS = 1e-05
CHUNK = 128
LAG = 1
MESH = pl.DeviceIdType.MESH
NEG = -1e30
SAFE = 64.0
VMEM = pltpu.VMEM


def spread(row):
    return jnp.broadcast_to(row, (HD, HD)).T


def project_kernel(
    side, count_ref, gap_ref, text_ref, visual_ref, gain_ref, wq_ref, wkv_ref,
    q_out, kv_out, lim_out, peak,
    before, scales, wsend, wall, seen, picked, landed, slots, lims, xall, psend_k, psend_q, pmid_k,
    pmid_q, precv_k, precv_q, squares, sqrecv, factors, qown,
    vis_s, vis_r, blk_s, blk_r, w_s, w_r, wp_s, wp_r, wr_s, wr_r, x_s, x_r, xf_s, xf_r, p_s, p_r, pf_s, pf_r,
    n_s, n_r, kx_s, kx_r, ky_s, ky_r, kc_s, kc_r, q_s, q_r,
):
    seq_count, enc_count = lax.axis_size("seq"), lax.axis_size("enc")
    s, e = lax.axis_index("seq"), lax.axis_index("enc")
    y, core, z, x = s // 2, s % 2, e // side, e % side
    ys = seq_count // 2
    rows, features = text_ref.shape
    chunks = rows // CHUNK
    window = landed.shape[1]
    vis_rows = seen.shape[1]
    q_columns, k_columns = psend_q.shape[2], psend_k.shape[2]
    psend, pmid, precv = (psend_k, psend_q), (pmid_k, pmid_q), (precv_k, precv_q)
    split = side * k_columns
    KEYS, QUERIES = 0, 1
    images = count_ref.shape[0]
    twin = s + 1 - 2 * core
    mate = e + 1 - 2 * (e % 2)
    other = seq_count - 1 - s
    sides = (1, side - 1)

    def across(k):
        return z * side + (x + k) % side

    def along(k):
        return ((z + k) % side) * side + x

    def column_of(k):
        return ((y + k) % ys) * 2 + core

    def send(source, target, ssem, rsem, to_s, to_e):
        return pltpu.make_async_remote_copy(
            src_ref=source, dst_ref=target, send_sem=ssem, recv_sem=rsem,
            device_id=(to_s, to_e), device_id_type=MESH,
        )

    seen[...] = jnp.zeros_like(seen)
    barrier = pltpu.get_barrier_semaphore()

    @pl.loop(1, enc_count)
    def _(k):
        pl.semaphore_signal(barrier, inc=1, device_id=(s, (e + k) % enc_count), device_id_type=MESH)

    @pl.loop(1, seq_count)
    def _(k):
        pl.semaphore_signal(barrier, inc=1, device_id=((s + k) % seq_count, e), device_id_type=MESH)

    pl.semaphore_wait(barrier, enc_count + seq_count - 2)

    def see(k):
        to = (e + k) % enc_count
        lanes = pl.ds(pl.multiple_of(to * features, features), features)
        there = seen.at[e, pl.ds(0, visual_ref.shape[0])]
        return send(visual_ref.at[:, lanes], there, vis_s.at[k], vis_r.at[k], s, to)

    for g in range(features // HD):
        scales[g * HD : (g + 1) * HD, :] = spread(
            gain_ref[g * HD : (g + 1) * HD].astype(jnp.float32).reshape(1, HD)
        )

    def scaled(ref, here, start):
        lanes = pl.ds(pl.multiple_of(start, HD), HD)
        return (ref[here, lanes].astype(jnp.float32) * scales[here, :]).astype(jnp.bfloat16)

    def gather_columns(target, here, to):
        for zz in range(side):
            owner = zz * side + to
            for j in range(q_columns // HD):
                target[:, pl.ds(split + zz * q_columns + j * HD, HD)] = scaled(
                    wq_ref, here, owner * q_columns + j * HD
                )
            for j in range(k_columns // HD):
                target[:, pl.ds(zz * k_columns + j * HD, HD)] = scaled(
                    wkv_ref, here, owner * k_columns + j * HD
                )

    deep = features // seq_count

    def part_of(owner):
        return pl.ds(pl.multiple_of(owner * deep, deep), deep)

    def weigh(k):
        return send(
            wsend.at[(x + k) % side], wall.at[x, part_of(s)], w_s.at[k], w_r.at[k], s, across(k)
        )

    def pass_weights(k, j):
        here = wall.at[(x + side - k) % side, part_of(s)]
        goal = twin if j == 0 else column_of(j)
        return send(here, here, wp_s.at[k, j], wp_r.at[k, j], goal, e)

    def relay_weights(k, j):
        here = wall.at[(x + side - k) % side, part_of(column_of(ys - j))]
        return send(here, here, wr_s.at[k, j], wr_r.at[k, j], twin, e)

    def pass_all(k):
        weigh(k).wait_recv()
        for j in range(1, ys):
            pass_weights(k, j).start()
        pass_weights(k, 0).start()

    @pl.loop(1, side)
    def _(k):
        to = (x + k) % side
        gather_columns(wsend.at[to], part_of(s), to)

    for k in sides:
        weigh(k).start()

    @pl.loop(1, enc_count)
    def _(k):
        see(k).start()

    for k in range(2, side - 1):
        weigh(k).start()

    kept = pltpu.make_async_copy(
        visual_ref.at[:, pl.ds(pl.multiple_of(e * features, features), features)],
        seen.at[e, pl.ds(0, visual_ref.shape[0])],
        vis_s.at[0],
    )
    kept.start()

    for g in range(features // HD):
        gather_columns(wall.at[x, pl.ds(g * HD, HD)], pl.ds(g * HD, HD), x)

    shape = slots.shape
    position = (
        s * rows
        + lax.broadcasted_iota(jnp.int32, shape, 0) * CHUNK
        + lax.broadcasted_iota(jnp.int32, shape, 1)
    )

    seat = jnp.where(
        lax.broadcasted_iota(jnp.int32, shape, 0) >= chunks // 2, position, position + (other - s) * rows
    )

    def place(i, carry):
        end, offset, shift, lim, counts = carry
        start = end + gap_ref[i]
        count = count_ref[i]
        end = start + count
        inside = (position >= start) & (position < end)
        shift = jnp.where(inside, offset - start, shift)
        lim = jnp.where((seat >= start) & (seat < end), end - 1, lim)
        counts = tuple(
            total + jnp.minimum(jnp.maximum(b * rows - start, 0), count)
            for b, total in enumerate(counts)
        )
        return end, offset + count, shift, lim, counts

    none = jnp.full(shape, 1, jnp.int32)
    zero = jnp.int32(0)
    _, _, shift, lim, counts = lax.fori_loop(
        0, images, place, (zero, zero, none, seat, (zero,) * seq_count)
    )
    for b in range(seq_count):
        before[b] = counts[b]
    lims[...] = lim.astype(jnp.float32)
    token = position + shift
    origin = (token // enc_count) % seq_count
    total = before[s]
    group = seq_count * enc_count
    skipped = (total // group) * enc_count + jnp.clip(total % group - enc_count * origin, 0, enc_count)
    slot = origin * window + (token // group) * enc_count + token % enc_count - skipped
    slots[...] = jnp.where(shift <= 0, slot, -1).astype(jnp.float32)

    for k in sides:
        pass_all(k)

    @pl.loop(1, enc_count)
    def _(k):
        see(k).wait_recv()

    kept.wait()

    def one_hot(index, count):
        lane = lax.broadcasted_iota(jnp.int32, index.shape, 1).astype(jnp.float32)
        return jnp.concatenate(
            [jnp.where(index == lane + j * HD, 1.0, 0.0).astype(jnp.bfloat16) for j in range(count // HD)],
            axis=1,
        )

    def pick(b):
        total = before[b]
        skip = (total // group) * enc_count + jnp.clip(total % group - enc_count * s, 0, enc_count)
        local = skip + lax.broadcasted_iota(jnp.int32, (window, HD), 0)
        index = (local % enc_count) * vis_rows + local // enc_count
        chosen = one_hot(index.astype(jnp.float32), enc_count * vis_rows)
        table = seen[...].reshape(enc_count * vis_rows, features)
        return jnp.dot(chosen, table, preferred_element_type=jnp.float32).astype(jnp.bfloat16)

    def move(k):
        to = (s + k) % seq_count
        return send(picked.at[to], landed.at[s], blk_s.at[k], blk_r.at[k], to, e)

    @pl.loop(1, seq_count)
    def _(k):
        to = (s + k) % seq_count
        picked[to] = pick(to)
        move(k).start()

    landed[s] = pick(s)

    for k in range(2, side - 1):
        pass_all(k)

    @pl.loop(1, seq_count)
    def _(k):
        move(k).wait_recv()

    def at(c):
        return pl.ds(pl.multiple_of(c * CHUNK, CHUNK), CHUNK)

    def half_of(k, c):
        return pl.ds(pl.multiple_of(c * CHUNK + (k // 2) * (CHUNK // 2), CHUNK // 2), CHUNK // 2)

    def share(k, c):
        return send(xall.at[x, at(c)], xall.at[x, at(c)], x_s.at[k, c], x_r.at[k, c], s, across(k))

    def relay(k, c):
        here = xall.at[(x + side - k) % side, half_of(k, c)]
        return send(here, here, xf_s.at[k, c], xf_r.at[k, c], s, across(k))

    def reach(kind, k, c):
        return send(
            psend[kind].at[(z + side // 2) % side, half_of(k, c)], pmid[kind].at[half_of(k, c)],
            pf_s.at[kind, k, c], pf_r.at[kind, k, c], s, along(k),
        )

    def reduce(kind, k, c):
        return send(
            psend[kind].at[(z + k) % side, at(c)], precv[kind].at[k // 2, at(c)],
            p_s.at[kind, k, c], p_r.at[kind, k, c], s, along(k),
        )

    def trade(c):
        return send(qown.at[at(c)], q_out.at[at(c)], q_s.at[c], q_r.at[c], other, e)

    def norms(k, c):
        return send(squares.at[c], sqrecv.at[k, c], n_s.at[k, c], n_r.at[k, c], s, along(k))

    def keys(owner, c):
        return pl.ds(pl.multiple_of(owner * rows + c * CHUNK, CHUNK), CHUNK)

    def pair(c):
        here = kv_out.at[e % 2, keys(s, c)]
        return send(here, here, kx_s.at[c], kx_r.at[c], s, mate)

    def column(k, c):
        here = kv_out.at[:, keys(s, c)]
        return send(here, here, ky_s.at[k, c], ky_r.at[k, c], column_of(k), e)

    def chip(k, c):
        here = kv_out.at[:, keys(column_of(ys - k), c)]
        return send(here, here, kc_s.at[k, c], kc_r.at[k, c], twin, e)

    ones = jnp.ones((8, side * features), jnp.bfloat16)

    def push(c):
        index = spread(slots[pl.ds(c, 1), :])
        chosen = one_hot(index, landed.shape[0] * window)
        table = landed[...].reshape(landed.shape[0] * window, features)
        frame = jnp.dot(chosen, table, preferred_element_type=jnp.float32).astype(jnp.bfloat16)
        visual = jnp.concatenate([index] * (features // HD), axis=1) >= 0
        xall[x, at(c)] = jnp.where(visual, frame, text_ref[at(c), :])
        lim_out[at(c), :] = spread(lims[pl.ds(c, 1), :])
        for k in sides:
            share(k, c).start()

    def hop(c):
        for k in sides:
            share(k, c).wait_recv()
            relay(k, c).start()

    def multiply(c):
        @pl.when(c == 0)
        def _():
            for k in range(1, side):
                for j in range(1, ys):
                    pass_weights(k, j).wait_recv()
                    relay_weights(k, j).start()
            for k in range(1, side):
                pass_weights(k, 0).wait_recv()
                for j in range(1, ys):
                    relay_weights(k, j).wait_recv()

        for k in sides:
            relay(k, c).wait_recv()
        block = jnp.concatenate([xall[j, at(c)] for j in range(side)], axis=1)
        wide = block.astype(jnp.float32)
        squares[c] = lax.dot_general(
            ones, (wide * wide).astype(jnp.bfloat16), (((1,), (1,)), ((), ())),
            preferred_element_type=jnp.float32,
        )
        for k in range(1, side):
            norms(k, c).start()
        launch(KEYS, c, block, 0, split)

    def launch(kind, c, block, start, stop):
        weights = wall[:, :, start:stop].reshape(side * features, stop - start)
        partial = jnp.dot(block, weights, preferred_element_type=jnp.float32).astype(jnp.bfloat16)
        width = (stop - start) // side
        for zz in range(side):
            psend[kind][zz, at(c)] = partial[:, zz * width : (zz + 1) * width]
        for k in sides:
            reach(kind, k, c).start()

    def multiply_queries(c):
        block = jnp.concatenate([xall[j, at(c)] for j in range(side)], axis=1)
        launch(QUERIES, c, block, split, split + side * q_columns)

    def merge(kind, c):
        for k in sides:
            reach(kind, k, c).wait_recv()
            here = half_of(k, c)
            target = (z + k) % side
            joined = psend[kind][target, here].astype(jnp.float32) + pmid[kind][here].astype(jnp.float32)
            psend[kind][target, here] = joined.astype(jnp.bfloat16)
            reduce(kind, k, c).start()

    def total_of(kind, c):
        total = psend[kind][z, at(c)].astype(jnp.float32)
        for k in sides:
            reduce(kind, k, c).wait_recv()
            total = total + precv[kind][k // 2, at(c)].astype(jnp.float32)
        return total

    def record(i, norm):
        wide = jnp.broadcast_to(norm, (CHUNK, HD)).reshape(CHUNK // 8, 8, HD)
        peak[i] = jnp.maximum(peak[i], jnp.max(wide, axis=0))

    def finish_keys(c):
        total = total_of(KEYS, c)
        square = squares[c]
        for k in range(1, side):
            norms(k, c).wait_recv()
            square = square + sqrecv[k, c]
        scale = spread(lax.rsqrt(square / (features * enc_count) + EPS)[0:1, :])
        factors[at(c), :] = scale * (math.log2(math.e) / HD**0.5)
        held = (total * scale).astype(jnp.bfloat16)
        kv_out[e % 2, keys(s, c)] = held
        pair(c).start()
        held = held.astype(jnp.float32)
        norm = jnp.sum(held * held, axis=1, keepdims=True)
        record(1, norm * (1 - e % 2).astype(jnp.float32))

    def finish_queries(c):
        total = total_of(QUERIES, c)
        norm = jnp.zeros((CHUNK, 1), jnp.float32)
        for j in range(q_columns // HD):
            lanes = slice(j * HD, (j + 1) * HD)
            asked = (total[:, lanes] * factors[at(c), :]).astype(jnp.bfloat16)
            qown[at(c), lanes] = asked
            asked = asked.astype(jnp.float32)
            norm = jnp.maximum(norm, jnp.sum(asked * asked, axis=1, keepdims=True))

        @pl.when(c >= chunks // 2)
        def _():
            q_out[at(c), :] = qown[at(c), :]

        @pl.when(c < chunks // 2)
        def _():
            trade(c).start()

        record(0, norm)

    def spread_out(c):
        pair(c).wait_recv()
        for k in range(1, ys):
            column(k, c).start()
        chip(0, c).start()

    def hand_over(c):
        for k in range(1, ys):
            column(k, c).wait_recv()
            chip(k, c).start()

    behind = LAG
    stages = (
        push, hop, multiply, multiply_queries, functools.partial(merge, KEYS),
        functools.partial(merge, QUERIES), finish_keys, spread_out, finish_queries, hand_over,
    )
    lags = (0, 2, 3, 3 + behind, 4, 4 + behind, 5, 6, 5 + behind, 8)
    peak[...] = jnp.zeros_like(peak)

    @pl.loop(0, chunks + max(lags))
    def _(t):
        for stage, lag in zip(stages, lags):
            @pl.when((t >= lag) & (t < chunks + lag))
            def _():
                stage(t - lag)

    @pl.loop(0, chunks)
    def _(c):
        pair(c).wait_send()
        chip(0, c).wait()
        for k in range(1, ys):
            chip(k, c).wait()
            column(k, c).wait_send()
        for k in sides:
            share(k, c).wait_send()
            relay(k, c).wait_send()
            for kind in (KEYS, QUERIES):
                reach(kind, k, c).wait_send()
                reduce(kind, k, c).wait_send()
        for k in range(1, side):
            norms(k, c).wait_send()

    @pl.loop(0, chunks // 2)
    def _(c):
        trade(c).wait()

    @pl.loop(1, side)
    def _(k):
        weigh(k).wait_send()
        for j in range(ys):
            pass_weights(k, j).wait_send()
        for j in range(1, ys):
            relay_weights(k, j).wait_send()

    @pl.loop(1, enc_count)
    def _(k):
        see(k).wait_send()

    @pl.loop(1, seq_count)
    def _(k):
        move(k).wait_send()


def project(text, visual, gain, w_query, w_keyval, image_count, text_gap):
    rows, features = text.shape
    vis_rows = pl.cdiv(visual.shape[0], 16) * 16
    seq_count, enc_count = lax.axis_size("seq"), lax.axis_size("enc")
    side, ys = math.isqrt(enc_count), seq_count // 2
    q_columns = w_query.shape[1] // enc_count
    columns = q_columns + w_keyval.shape[1] // enc_count
    chunks = rows // CHUNK
    window = rows // seq_count
    bf16, f32 = jnp.bfloat16, jnp.float32

    def dma(*shape):
        return [pltpu.SemaphoreType.DMA(shape)] * 2

    return pl.pallas_call(
        functools.partial(project_kernel, side),
        out_shape=(
            jax.ShapeDtypeStruct((rows, q_columns), bf16),
            jax.ShapeDtypeStruct((2, rows * seq_count, HD), bf16),
            jax.ShapeDtypeStruct((rows, HD), f32),
            jax.ShapeDtypeStruct((2, 8, HD), f32),
        ),
        in_specs=[pl.BlockSpec(memory_space=pltpu.SMEM)] * 2
        + [pl.BlockSpec(memory_space=VMEM), pl.BlockSpec(memory_space=pl.ANY)]
        + [pl.BlockSpec(memory_space=VMEM)] * 3,
        out_specs=tuple([pl.BlockSpec(memory_space=VMEM)] * 4),
        scratch_shapes=[
            pltpu.SMEM((seq_count,), jnp.int32),
            VMEM((features, HD), f32),
            VMEM((side, features // seq_count, side * columns), bf16),
            VMEM((side, features, side * columns), bf16),
            VMEM((enc_count, vis_rows, features), bf16),
            VMEM((seq_count, window, features), bf16),
            VMEM((seq_count, window, features), bf16),
            VMEM((16, HD), f32),
            VMEM((16, HD), f32),
            VMEM((side, rows, features), bf16),
            VMEM((side, rows, columns - q_columns), bf16),
            VMEM((side, rows, q_columns), bf16),
            VMEM((rows, columns - q_columns), bf16),
            VMEM((rows, q_columns), bf16),
            VMEM((2, rows, columns - q_columns), bf16),
            VMEM((2, rows, q_columns), bf16),
            VMEM((chunks, 8, CHUNK), f32),
            VMEM((side, chunks, 8, CHUNK), f32),
            VMEM((rows, HD), f32),
            VMEM((rows, q_columns), bf16),
            *dma(enc_count),
            *dma(seq_count),
            *dma(side),
            *dma(side, ys),
            *dma(side, ys),
            *dma(side, chunks),
            *dma(side, chunks),
            *dma(2, side, chunks),
            *dma(2, side, chunks),
            *dma(side, chunks),
            *dma(chunks),
            *dma(ys, chunks),
            *dma(ys, chunks),
            *dma(chunks),
        ],
        compiler_params=pltpu.CompilerParams(
            collective_id=0, has_side_effects=True, vmem_limit_bytes=60 << 20
        ),
    )(image_count, text_gap, text, visual, gain, w_query, w_keyval)


def masked_scores(q, keys, lim, key):
    s = lax.dot_general(q, keys, (((1,), (1,)), ((), ())), preferred_element_type=jnp.float32)
    if lim is None:
        return s
    at = (key + lax.broadcasted_iota(jnp.int32, s.shape, 1)).astype(jnp.float32)
    return jnp.where(at <= jnp.concatenate([lim] * (s.shape[1] // HD), axis=1), s, NEG)


def lane_sums(p):
    total = p[:, :HD]
    for part in range(1, p.shape[1] // HD):
        total = total + p[:, part * HD : (part + 1) * HD]
    return total


def quick_kernel(
    bk, side, q_ref, kv_ref, lim_ref, top_ref, o_ref, safe_ref,
    kv, lent, acc, den, peak, peaks, kv_s, o_s, o_r, m_s, m_r,
):
    s, e = lax.axis_index("seq"), lax.axis_index("enc")
    seq_count = lax.axis_size("seq")
    other = seq_count - 1 - s
    heads = q_ref.shape[1] // HD
    rows = q_ref.shape[0]
    half = rows // 2
    blocks = kv_ref.shape[1] // bk

    def load(j):
        here = pl.ds(pl.multiple_of(j * bk, bk), bk)
        return pltpu.make_async_copy(kv_ref.at[:, here], kv.at[:, here], kv_s.at[j])

    @pl.loop(0, blocks)
    def _(j):
        load(j).start()

    barrier = pltpu.get_barrier_semaphore()
    z, x = e // side, e % side
    sizes = (side, side, seq_count)

    def goal(step, k):
        if step == 0:
            return s, z * side + (x + k) % side
        if step == 1:
            return s, ((z + k) % side) * side + x
        return (s + k) % seq_count, e

    for step, size in enumerate(sizes):
        for k in range(1, size):
            pl.semaphore_signal(barrier, inc=1, device_id=goal(step, k), device_id_type=MESH)

    peak[0] = top_ref[...]

    def meet(step, k):
        return pltpu.make_async_remote_copy(
            src_ref=peak.at[step], dst_ref=peaks.at[step, k], send_sem=m_s.at[step, k],
            recv_sem=m_r.at[step, k], device_id=goal(step, k), device_id_type=MESH,
        )

    def climb(step):
        if step > 0:
            highest = peak[step - 1]
            for k in range(1, sizes[step - 1]):
                meet(step - 1, k).wait_recv()
                highest = jnp.maximum(highest, peaks[step - 1, k])
            if step == len(sizes):
                bound = jnp.max(highest[0]) * jnp.max(highest[1])
                safe_ref[0] = jnp.where(bound < SAFE * SAFE, 1, 0).astype(jnp.int32)
                return
            peak[step] = highest
        for k in range(1, sizes[step]):
            meet(step, k).start()

    def job(part, first, ready, target, base, hook):
        size = half
        rows_here = pl.ds(part * half, half)
        acc[...] = jnp.zeros_like(acc)
        den[...] = jnp.zeros_like(den)
        whole = first // bk
        last = jnp.minimum((first + size + 255 + bk - 1) // bk, blocks)

        def step(j, masked):
            @pl.when(j >= ready)
            def _():
                load(j).wait()

            key = pl.multiple_of(j * bk, bk)
            keys, values = kv[0, pl.ds(key, bk), :], kv[1, pl.ds(key, bk), :]
            lim = lim_ref[rows_here, :] if masked else None
            for head in range(heads):
                q = q_ref[rows_here, head * HD : (head + 1) * HD]
                p = jnp.exp2(masked_scores(q, keys, lim, key))
                acc[head] += jnp.dot(
                    p.astype(jnp.bfloat16), values, preferred_element_type=jnp.float32
                )
                den[head] += lane_sums(p)

        @pl.loop(0, whole)
        def _(j):
            step(j, False)

        hook(1)

        @pl.loop(whole, last)
        def _(j):
            step(j, True)

        hook(2)
        for head in range(heads):
            result = acc[head] / jnp.sum(den[head], axis=1, keepdims=True)
            target[base : base + half, head * HD : (head + 1) * HD] = result.astype(jnp.bfloat16)
        return last

    used = job(0, other * rows, 0, lent, 0, lambda step: None)
    pl.semaphore_wait(barrier, sum(sizes) - len(sizes))
    back = pltpu.make_async_remote_copy(
        src_ref=lent, dst_ref=o_ref.at[pl.ds(0, half)], send_sem=o_s, recv_sem=o_r,
        device_id=(other, e), device_id_type=MESH,
    )
    back.start()
    climb(0)
    used = jnp.maximum(used, job(1, s * rows + half, used, o_ref, half, climb))

    @pl.loop(used, blocks)
    def _(j):
        load(j).wait()

    climb(3)
    back.wait()
    for step, size in enumerate(sizes):
        for k in range(1, size):
            meet(step, k).wait_send()


def quick(query, keyval, lim, peak):
    rows, width = query.shape
    seq_count = lax.axis_size("seq")
    side = math.isqrt(lax.axis_size("enc"))
    heads, bk = width // HD, 1024
    return pl.pallas_call(
        functools.partial(quick_kernel, bk, side),
        out_shape=(
            jax.ShapeDtypeStruct((rows, width), jnp.bfloat16),
            jax.ShapeDtypeStruct((1,), jnp.int32),
        ),
        in_specs=[
            pl.BlockSpec(memory_space=VMEM),
            pl.BlockSpec(memory_space=pl.ANY),
            pl.BlockSpec(memory_space=VMEM),
            pl.BlockSpec(memory_space=VMEM),
        ],
        out_specs=(pl.BlockSpec(memory_space=VMEM), pl.BlockSpec(memory_space=pltpu.SMEM)),
        scratch_shapes=[
            VMEM(keyval.shape, jnp.bfloat16),
            VMEM((rows // 2, width), jnp.bfloat16),
            VMEM((heads, rows // 2, HD), jnp.float32),
            VMEM((heads, rows // 2, HD), jnp.float32),
            VMEM((3, 2, 8, HD), jnp.float32),
            VMEM((3, seq_count, 2, 8, HD), jnp.float32),
            pltpu.SemaphoreType.DMA((keyval.shape[1] // bk,)),
            pltpu.SemaphoreType.DMA,
            pltpu.SemaphoreType.DMA,
            pltpu.SemaphoreType.DMA((3, seq_count)),
            pltpu.SemaphoreType.DMA((3, seq_count)),
        ],
        compiler_params=pltpu.CompilerParams(
            collective_id=1, has_side_effects=True, vmem_limit_bytes=56 << 20
        ),
    )(query, keyval, lim, peak)


def careful_kernel(bq, bk, off_ref, q_ref, kv_ref, lim_ref, o_ref, acc, den, top):
    heads = q_ref.shape[1] // HD

    @pl.loop(0, q_ref.shape[0] // bq)
    def _(tile):
        row = pl.multiple_of(tile * bq, bq)
        acc[...] = jnp.zeros_like(acc)
        den[...] = jnp.zeros_like(den)
        top[...] = jnp.full_like(top, NEG)
        last = jnp.minimum(pl.cdiv(off_ref[0] + row + bq + 255, bk), kv_ref.shape[1] // bk)

        @pl.loop(0, last)
        def _(j):
            key = pl.multiple_of(j * bk, bk)
            keys, values = kv_ref[0, pl.ds(key, bk), :], kv_ref[1, pl.ds(key, bk), :]
            for head in range(heads):
                q = q_ref[pl.ds(row, bq), head * HD : (head + 1) * HD]
                s = masked_scores(q, keys, lim_ref[pl.ds(row, bq), :], key)
                old = top[head]
                new = jnp.maximum(old, jnp.max(s, axis=1, keepdims=True))
                top[head] = new
                p = jnp.exp2(s - new)
                shrink = jnp.exp2(old - new)
                acc[head] = acc[head] * shrink + jnp.dot(
                    p.astype(jnp.bfloat16), values, preferred_element_type=jnp.float32
                )
                den[head] = den[head] * shrink + lane_sums(p)

        for head in range(heads):
            result = acc[head] / jnp.sum(den[head], axis=1, keepdims=True)
            o_ref[pl.ds(row, bq), head * HD : (head + 1) * HD] = result.astype(jnp.bfloat16)


def careful(query, keyval, lim):
    rows, width = query.shape
    half, heads, bq, bk = rows // 2, width // HD, 128, 512
    seq_count = lax.axis_size("seq")
    mine = (lax.axis_index("seq") * rows).astype(jnp.int32)
    theirs = (seq_count - 1) * rows - mine

    def attend(q0, part):
        return pl.pallas_call(
            functools.partial(careful_kernel, bq, bk),
            out_shape=jax.ShapeDtypeStruct((half, width), jnp.bfloat16),
            grid=(1,),
            in_specs=[
                pl.BlockSpec(memory_space=pltpu.SMEM),
                pl.BlockSpec((half, width), lambda i: (part, 0)),
                pl.BlockSpec(memory_space=VMEM),
                pl.BlockSpec((half, HD), lambda i: (part, 0)),
            ],
            out_specs=pl.BlockSpec(memory_space=VMEM),
            scratch_shapes=[
                VMEM((heads, bq, HD), jnp.float32),
                VMEM((heads, bq, HD), jnp.float32),
                VMEM((heads, bq, 1), jnp.float32),
            ],
            compiler_params=pltpu.CompilerParams(vmem_limit_bytes=56 << 20),
        )(q0.reshape(1), query, keyval, lim)

    lent = attend(theirs, 0)
    back = lax.ppermute(lent, "seq", [(i, seq_count - 1 - i) for i in range(seq_count)])
    return jnp.concatenate((back, attend(mine + half, 1)), axis=0)


def per_device(text, visual, gain, w_query, w_keyval, image_count, text_gap):
    query, keyval, lim, peak = project(
        text, visual, gain, w_query, w_keyval, image_count, text_gap
    )
    attended, safe = quick(query, keyval, lim, peak)
    return lax.cond(
        safe[0] > 0,
        lambda done, *rest: done,
        lambda done, *rest: careful(*rest),
        attended, query, keyval, lim,
    )


def solution(mesh):
    in_specs = (
        P("seq", "enc"),
        P(("seq", "enc"), None),
        P("enc"),
        P("enc", None),
        P("enc", None),
        P(),
        P(),
    )
    out_specs = P("seq", "enc")
    return jax.shard_map(
        per_device, mesh=mesh, in_specs=in_specs, out_specs=out_specs, check_vma=False
    )
```

```python
import functools
import math

import jax
import jax.numpy as jnp
from jax import lax
from jax.experimental import pallas as pl
from jax.experimental.pallas import tpu as pltpu
from jax.sharding import PartitionSpec as P

HD = 128
EPS = 1e-05
CHUNK = 128
LAG = 0
MESH = pl.DeviceIdType.MESH
NEG = -1e30
SAFE = 64.0
VMEM = pltpu.VMEM


def spread(row):
    return jnp.broadcast_to(row, (HD, HD)).T


def project_kernel(
    side, count_ref, gap_ref, text_ref, visual_ref, gain_ref, wq_ref, wkv_ref,
    q_out, kv_out, lim_out, peak_out,
    before, scales, wsend, wall, seen, picked, landed, slots, lims, xall, psend_k, psend_q, pmid_k,
    pmid_q, precv_k, precv_q, squares, sqrecv, factors, qown, peak, peaks,
    vis_s, vis_r, blk_s, blk_r, w_s, w_r, wp_s, wp_r, wr_s, wr_r, x_s, x_r, xf_s, xf_r, p_s, p_r, pf_s, pf_r,
    n_s, n_r, kx_s, kx_r, ky_s, ky_r, kc_s, kc_r, q_s, q_r, m_s, m_r,
):
    seq_count, enc_count = lax.axis_size("seq"), lax.axis_size("enc")
    s, e = lax.axis_index("seq"), lax.axis_index("enc")
    y, core, z, x = s // 2, s % 2, e // side, e % side
    ys = seq_count // 2
    rows, features = text_ref.shape
    chunks = rows // CHUNK
    window = landed.shape[1]
    vis_rows = seen.shape[1]
    q_columns, k_columns = psend_q.shape[2], psend_k.shape[2]
    psend, pmid, precv = (psend_k, psend_q), (pmid_k, pmid_q), (precv_k, precv_q)
    split = side * k_columns
    KEYS, QUERIES = 0, 1
    images = count_ref.shape[0]
    twin = s + 1 - 2 * core
    mate = e + 1 - 2 * (e % 2)
    other = seq_count - 1 - s
    sides = (1, side - 1)

    def across(k):
        return z * side + (x + k) % side

    def along(k):
        return ((z + k) % side) * side + x

    def column_of(k):
        return ((y + k) % ys) * 2 + core

    def send(source, target, ssem, rsem, to_s, to_e):
        return pltpu.make_async_remote_copy(
            src_ref=source, dst_ref=target, send_sem=ssem, recv_sem=rsem,
            device_id=(to_s, to_e), device_id_type=MESH,
        )

    seen[...] = jnp.zeros_like(seen)
    barrier = pltpu.get_barrier_semaphore()

    @pl.loop(1, enc_count)
    def _(k):
        pl.semaphore_signal(barrier, inc=1, device_id=(s, (e + k) % enc_count), device_id_type=MESH)

    @pl.loop(1, seq_count)
    def _(k):
        pl.semaphore_signal(barrier, inc=1, device_id=((s + k) % seq_count, e), device_id_type=MESH)

    pl.semaphore_wait(barrier, enc_count + seq_count - 2)

    def see(k):
        to = (e + k) % enc_count
        lanes = pl.ds(pl.multiple_of(to * features, features), features)
        there = seen.at[e, pl.ds(0, visual_ref.shape[0])]
        return send(visual_ref.at[:, lanes], there, vis_s.at[k], vis_r.at[k], s, to)

    for g in range(features // HD):
        scales[g * HD : (g + 1) * HD, :] = spread(
            gain_ref[g * HD : (g + 1) * HD].astype(jnp.float32).reshape(1, HD)
        )

    def scaled(ref, here, start):
        lanes = pl.ds(pl.multiple_of(start, HD), HD)
        return (ref[here, lanes].astype(jnp.float32) * scales[here, :]).astype(jnp.bfloat16)

    def gather_columns(target, here, to):
        for zz in range(side):
            owner = zz * side + to
            for j in range(q_columns // HD):
                target[:, pl.ds(split + zz * q_columns + j * HD, HD)] = scaled(
                    wq_ref, here, owner * q_columns + j * HD
                )
            for j in range(k_columns // HD):
                target[:, pl.ds(zz * k_columns + j * HD, HD)] = scaled(
                    wkv_ref, here, owner * k_columns + j * HD
                )

    deep = features // seq_count

    def part_of(owner):
        return pl.ds(pl.multiple_of(owner * deep, deep), deep)

    def weigh(k):
        return send(
            wsend.at[(x + k) % side], wall.at[x, part_of(s)], w_s.at[k], w_r.at[k], s, across(k)
        )

    def pass_weights(k, j):
        here = wall.at[(x + side - k) % side, part_of(s)]
        goal = twin if j == 0 else column_of(j)
        return send(here, here, wp_s.at[k, j], wp_r.at[k, j], goal, e)

    def relay_weights(k, j):
        here = wall.at[(x + side - k) % side, part_of(column_of(ys - j))]
        return send(here, here, wr_s.at[k, j], wr_r.at[k, j], twin, e)

    def pass_all(k):
        weigh(k).wait_recv()
        for j in range(1, ys):
            pass_weights(k, j).start()
        pass_weights(k, 0).start()

    @pl.loop(1, side)
    def _(k):
        to = (x + k) % side
        gather_columns(wsend.at[to], part_of(s), to)

    for k in sides:
        weigh(k).start()

    @pl.loop(1, enc_count)
    def _(k):
        see(k).start()

    for k in range(2, side - 1):
        weigh(k).start()

    kept = pltpu.make_async_copy(
        visual_ref.at[:, pl.ds(pl.multiple_of(e * features, features), features)],
        seen.at[e, pl.ds(0, visual_ref.shape[0])],
        vis_s.at[0],
    )
    kept.start()

    for g in range(features // HD):
        gather_columns(wall.at[x, pl.ds(g * HD, HD)], pl.ds(g * HD, HD), x)

    shape = slots.shape
    position = (
        s * rows
        + lax.broadcasted_iota(jnp.int32, shape, 0) * CHUNK
        + lax.broadcasted_iota(jnp.int32, shape, 1)
    )

    seat = jnp.where(
        lax.broadcasted_iota(jnp.int32, shape, 0) >= chunks // 2, position, position + (other - s) * rows
    )

    def place(i, carry):
        end, offset, shift, lim, counts = carry
        start = end + gap_ref[i]
        count = count_ref[i]
        end = start + count
        inside = (position >= start) & (position < end)
        shift = jnp.where(inside, offset - start, shift)
        lim = jnp.where((seat >= start) & (seat < end), end - 1, lim)
        counts = tuple(
            total + jnp.minimum(jnp.maximum(b * rows - start, 0), count)
            for b, total in enumerate(counts)
        )
        return end, offset + count, shift, lim, counts

    none = jnp.full(shape, 1, jnp.int32)
    zero = jnp.int32(0)
    _, _, shift, lim, counts = lax.fori_loop(
        0, images, place, (zero, zero, none, seat, (zero,) * seq_count)
    )
    for b in range(seq_count):
        before[b] = counts[b]
    lims[...] = lim.astype(jnp.float32)
    token = position + shift
    origin = (token // enc_count) % seq_count
    total = before[s]
    group = seq_count * enc_count
    skipped = (total // group) * enc_count + jnp.clip(total % group - enc_count * origin, 0, enc_count)
    slot = origin * window + (token // group) * enc_count + token % enc_count - skipped
    slots[...] = jnp.where(shift <= 0, slot, -1).astype(jnp.float32)

    for k in sides:
        pass_all(k)

    @pl.loop(1, enc_count)
    def _(k):
        see(k).wait_recv()

    kept.wait()

    def one_hot(index, count):
        lane = lax.broadcasted_iota(jnp.int32, index.shape, 1).astype(jnp.float32)
        return jnp.concatenate(
            [jnp.where(index == lane + j * HD, 1.0, 0.0).astype(jnp.bfloat16) for j in range(count // HD)],
            axis=1,
        )

    def pick(b):
        total = before[b]
        skip = (total // group) * enc_count + jnp.clip(total % group - enc_count * s, 0, enc_count)
        local = skip + lax.broadcasted_iota(jnp.int32, (window, HD), 0)
        index = (local % enc_count) * vis_rows + local // enc_count
        chosen = one_hot(index.astype(jnp.float32), enc_count * vis_rows)
        table = seen[...].reshape(enc_count * vis_rows, features)
        return jnp.dot(chosen, table, preferred_element_type=jnp.float32).astype(jnp.bfloat16)

    def move(k):
        to = (s + k) % seq_count
        return send(picked.at[to], landed.at[s], blk_s.at[k], blk_r.at[k], to, e)

    @pl.loop(1, seq_count)
    def _(k):
        to = (s + k) % seq_count
        picked[to] = pick(to)
        move(k).start()

    landed[s] = pick(s)

    for k in range(2, side - 1):
        pass_all(k)

    @pl.loop(1, seq_count)
    def _(k):
        move(k).wait_recv()

    def at(c):
        return pl.ds(pl.multiple_of(c * CHUNK, CHUNK), CHUNK)

    def half_of(k, c):
        return pl.ds(pl.multiple_of(c * CHUNK + (k // 2) * (CHUNK // 2), CHUNK // 2), CHUNK // 2)

    def share(k, c):
        return send(xall.at[x, at(c)], xall.at[x, at(c)], x_s.at[k, c], x_r.at[k, c], s, across(k))

    def relay(k, c):
        here = xall.at[(x + side - k) % side, half_of(k, c)]
        return send(here, here, xf_s.at[k, c], xf_r.at[k, c], s, across(k))

    def reach(kind, k, c):
        return send(
            psend[kind].at[(z + side // 2) % side, half_of(k, c)], pmid[kind].at[half_of(k, c)],
            pf_s.at[kind, k, c], pf_r.at[kind, k, c], s, along(k),
        )

    def reduce(kind, k, c):
        return send(
            psend[kind].at[(z + k) % side, at(c)], precv[kind].at[k // 2, at(c)],
            p_s.at[kind, k, c], p_r.at[kind, k, c], s, along(k),
        )

    def trade(c):
        return send(qown.at[at(c)], q_out.at[at(c)], q_s.at[c], q_r.at[c], other, e)

    def norms(k, c):
        return send(squares.at[c], sqrecv.at[k, c], n_s.at[k, c], n_r.at[k, c], s, along(k))

    def keys(owner, c):
        return pl.ds(pl.multiple_of(owner * rows + c * CHUNK, CHUNK), CHUNK)

    def pair(c):
        here = kv_out.at[e % 2, keys(s, c)]
        return send(here, here, kx_s.at[c], kx_r.at[c], s, mate)

    def column(k, c):
        here = kv_out.at[:, keys(s, c)]
        return send(here, here, ky_s.at[k, c], ky_r.at[k, c], column_of(k), e)

    def chip(k, c):
        here = kv_out.at[:, keys(column_of(ys - k), c)]
        return send(here, here, kc_s.at[k, c], kc_r.at[k, c], twin, e)

    ones = jnp.ones((8, side * features), jnp.bfloat16)

    def push(c):
        index = spread(slots[pl.ds(c, 1), :])
        chosen = one_hot(index, landed.shape[0] * window)
        table = landed[...].reshape(landed.shape[0] * window, features)
        frame = jnp.dot(chosen, table, preferred_element_type=jnp.float32).astype(jnp.bfloat16)
        visual = jnp.concatenate([index] * (features // HD), axis=1) >= 0
        xall[x, at(c)] = jnp.where(visual, frame, text_ref[at(c), :])
        lim_out[at(c), :] = spread(lims[pl.ds(c, 1), :])
        for k in sides:
            share(k, c).start()

    def hop(c):
        for k in sides:
            share(k, c).wait_recv()
            relay(k, c).start()

    def multiply(c):
        @pl.when(c == 0)
        def _():
            for k in range(1, side):
                for j in range(1, ys):
                    pass_weights(k, j).wait_recv()
                    relay_weights(k, j).start()
            for k in range(1, side):
                pass_weights(k, 0).wait_recv()
                for j in range(1, ys):
                    relay_weights(k, j).wait_recv()

        for k in sides:
            relay(k, c).wait_recv()
        block = jnp.concatenate([xall[j, at(c)] for j in range(side)], axis=1)
        wide = block.astype(jnp.float32)
        squares[c] = lax.dot_general(
            ones, (wide * wide).astype(jnp.bfloat16), (((1,), (1,)), ((), ())),
            preferred_element_type=jnp.float32,
        )
        for k in range(1, side):
            norms(k, c).start()
        launch(KEYS, c, block, 0, split)

    def launch(kind, c, block, start, stop):
        weights = wall[:, :, start:stop].reshape(side * features, stop - start)
        partial = jnp.dot(block, weights, preferred_element_type=jnp.float32).astype(jnp.bfloat16)
        width = (stop - start) // side
        for zz in range(side):
            psend[kind][zz, at(c)] = partial[:, zz * width : (zz + 1) * width]
        for k in sides:
            reach(kind, k, c).start()

    def multiply_queries(c):
        block = jnp.concatenate([xall[j, at(c)] for j in range(side)], axis=1)
        launch(QUERIES, c, block, split, split + side * q_columns)

    def merge(kind, c):
        for k in sides:
            reach(kind, k, c).wait_recv()
            here = half_of(k, c)
            target = (z + k) % side
            joined = psend[kind][target, here].astype(jnp.float32) + pmid[kind][here].astype(jnp.float32)
            psend[kind][target, here] = joined.astype(jnp.bfloat16)
            reduce(kind, k, c).start()

    def total_of(kind, c):
        total = psend[kind][z, at(c)].astype(jnp.float32)
        for k in sides:
            reduce(kind, k, c).wait_recv()
            total = total + precv[kind][k // 2, at(c)].astype(jnp.float32)
        return total

    def record(i, norm):
        wide = jnp.broadcast_to(norm, (CHUNK, HD)).reshape(CHUNK // 8, 8, HD)
        peak[0, i] = jnp.maximum(peak[0, i], jnp.max(wide, axis=0))

    def meet(step, k):
        return send(
            peak.at[step], peaks.at[step, k], m_s.at[step, k], m_r.at[step, k],
            s, along(k) if step else across(k),
        )

    def climb(step, c):
        @pl.when(c == chunks - 1)
        def _():
            if step > 0:
                highest = peak[step - 1]
                for k in range(1, side):
                    meet(step - 1, k).wait_recv()
                    highest = jnp.maximum(highest, peaks[step - 1, k])
                if step == 2:
                    peak_out[...] = highest
                    return
                peak[step] = highest
            for k in range(1, side):
                meet(step, k).start()

    def finish_keys(c):
        total = total_of(KEYS, c)
        square = squares[c]
        for k in range(1, side):
            norms(k, c).wait_recv()
            square = square + sqrecv[k, c]
        scale = spread(lax.rsqrt(square / (features * enc_count) + EPS)[0:1, :])
        factors[at(c), :] = scale * (math.log2(math.e) / HD**0.5)
        held = (total * scale).astype(jnp.bfloat16)
        kv_out[e % 2, keys(s, c)] = held
        pair(c).start()
        held = held.astype(jnp.float32)
        norm = jnp.sum(held * held, axis=1, keepdims=True)
        record(1, norm * (1 - e % 2).astype(jnp.float32))

    def finish_queries(c):
        total = total_of(QUERIES, c)
        norm = jnp.zeros((CHUNK, 1), jnp.float32)
        for j in range(q_columns // HD):
            lanes = slice(j * HD, (j + 1) * HD)
            asked = (total[:, lanes] * factors[at(c), :]).astype(jnp.bfloat16)
            qown[at(c), lanes] = asked
            asked = asked.astype(jnp.float32)
            norm = jnp.maximum(norm, jnp.sum(asked * asked, axis=1, keepdims=True))

        @pl.when(c >= chunks // 2)
        def _():
            q_out[at(c), :] = qown[at(c), :]

        @pl.when(c < chunks // 2)
        def _():
            trade(c).start()

        record(0, norm)

    def spread_out(c):
        pair(c).wait_recv()
        for k in range(1, ys):
            column(k, c).start()
        chip(0, c).start()

    def hand_over(c):
        for k in range(1, ys):
            column(k, c).wait_recv()
            chip(k, c).start()

    behind = LAG
    stages = (
        push, hop, multiply, multiply_queries, functools.partial(merge, KEYS),
        functools.partial(merge, QUERIES), finish_keys, spread_out, finish_queries,
        functools.partial(climb, 0), functools.partial(climb, 1), hand_over,
        functools.partial(climb, 2),
    )
    lags = (0, 2, 3, 3 + behind, 4, 4 + behind, 5, 6, 5 + behind, 5 + behind, 6 + behind, 8, 8)
    peak[...] = jnp.zeros_like(peak)

    @pl.loop(0, chunks + max(lags))
    def _(t):
        for stage, lag in zip(stages, lags):
            @pl.when((t >= lag) & (t < chunks + lag))
            def _():
                stage(t - lag)

    @pl.loop(0, chunks)
    def _(c):
        pair(c).wait_send()
        chip(0, c).wait()
        for k in range(1, ys):
            chip(k, c).wait()
            column(k, c).wait_send()
        for k in sides:
            share(k, c).wait_send()
            relay(k, c).wait_send()
            for kind in (KEYS, QUERIES):
                reach(kind, k, c).wait_send()
                reduce(kind, k, c).wait_send()
        for k in range(1, side):
            norms(k, c).wait_send()

    @pl.loop(0, chunks // 2)
    def _(c):
        trade(c).wait()

    for step in range(2):
        for k in range(1, side):
            meet(step, k).wait_send()

    @pl.loop(1, side)
    def _(k):
        weigh(k).wait_send()
        for j in range(ys):
            pass_weights(k, j).wait_send()
        for j in range(1, ys):
            relay_weights(k, j).wait_send()

    @pl.loop(1, enc_count)
    def _(k):
        see(k).wait_send()

    @pl.loop(1, seq_count)
    def _(k):
        move(k).wait_send()


def project(text, visual, gain, w_query, w_keyval, image_count, text_gap):
    rows, features = text.shape
    vis_rows = pl.cdiv(visual.shape[0], 16) * 16
    seq_count, enc_count = lax.axis_size("seq"), lax.axis_size("enc")
    side, ys = math.isqrt(enc_count), seq_count // 2
    q_columns = w_query.shape[1] // enc_count
    columns = q_columns + w_keyval.shape[1] // enc_count
    chunks = rows // CHUNK
    window = rows // seq_count
    bf16, f32 = jnp.bfloat16, jnp.float32

    def dma(*shape):
        return [pltpu.SemaphoreType.DMA(shape)] * 2

    return pl.pallas_call(
        functools.partial(project_kernel, side),
        out_shape=(
            jax.ShapeDtypeStruct((rows, q_columns), bf16),
            jax.ShapeDtypeStruct((2, rows * seq_count, HD), bf16),
            jax.ShapeDtypeStruct((rows, HD), f32),
            jax.ShapeDtypeStruct((2, 8, HD), f32),
        ),
        in_specs=[pl.BlockSpec(memory_space=pltpu.SMEM)] * 2
        + [pl.BlockSpec(memory_space=VMEM), pl.BlockSpec(memory_space=pl.ANY)]
        + [pl.BlockSpec(memory_space=VMEM)] * 3,
        out_specs=tuple([pl.BlockSpec(memory_space=VMEM)] * 4),
        scratch_shapes=[
            pltpu.SMEM((seq_count,), jnp.int32),
            VMEM((features, HD), f32),
            VMEM((side, features // seq_count, side * columns), bf16),
            VMEM((side, features, side * columns), bf16),
            VMEM((enc_count, vis_rows, features), bf16),
            VMEM((seq_count, window, features), bf16),
            VMEM((seq_count, window, features), bf16),
            VMEM((16, HD), f32),
            VMEM((16, HD), f32),
            VMEM((side, rows, features), bf16),
            VMEM((side, rows, columns - q_columns), bf16),
            VMEM((side, rows, q_columns), bf16),
            VMEM((rows, columns - q_columns), bf16),
            VMEM((rows, q_columns), bf16),
            VMEM((2, rows, columns - q_columns), bf16),
            VMEM((2, rows, q_columns), bf16),
            VMEM((chunks, 8, CHUNK), f32),
            VMEM((side, chunks, 8, CHUNK), f32),
            VMEM((rows, HD), f32),
            VMEM((rows, q_columns), bf16),
            VMEM((2, 2, 8, HD), f32),
            VMEM((2, side, 2, 8, HD), f32),
            *dma(enc_count),
            *dma(seq_count),
            *dma(side),
            *dma(side, ys),
            *dma(side, ys),
            *dma(side, chunks),
            *dma(side, chunks),
            *dma(2, side, chunks),
            *dma(2, side, chunks),
            *dma(side, chunks),
            *dma(chunks),
            *dma(ys, chunks),
            *dma(ys, chunks),
            *dma(chunks),
            *dma(2, side),
        ],
        compiler_params=pltpu.CompilerParams(
            collective_id=0, has_side_effects=True, vmem_limit_bytes=60 << 20
        ),
    )(image_count, text_gap, text, visual, gain, w_query, w_keyval)


def masked_scores(q, keys, lim, key):
    s = lax.dot_general(q, keys, (((1,), (1,)), ((), ())), preferred_element_type=jnp.float32)
    if lim is None:
        return s
    at = (key + lax.broadcasted_iota(jnp.int32, s.shape, 1)).astype(jnp.float32)
    return jnp.where(at <= jnp.concatenate([lim] * (s.shape[1] // HD), axis=1), s, NEG)


def lane_sums(p):
    total = p[:, :HD]
    for part in range(1, p.shape[1] // HD):
        total = total + p[:, part * HD : (part + 1) * HD]
    return total


def quick_kernel(
    bk, cuts, q_ref, kv_ref, lim_ref, top_ref, o_ref, safe_ref,
    kv, lent, acc, den, peaks, kv_s, o_s, o_r, m_s, m_r,
):
    s, e = lax.axis_index("seq"), lax.axis_index("enc")
    seq_count = lax.axis_size("seq")
    other = seq_count - 1 - s
    heads = q_ref.shape[1] // HD
    rows = q_ref.shape[0]
    half = rows // 2
    blocks = kv_ref.shape[1] // bk

    def load(j):
        here = pl.ds(pl.multiple_of(j * bk, bk), bk)
        return pltpu.make_async_copy(kv_ref.at[:, here], kv.at[:, here], kv_s.at[j])

    @pl.loop(0, blocks)
    def _(j):
        load(j).start()

    barrier = pltpu.get_barrier_semaphore()

    @pl.loop(1, seq_count)
    def _(k):
        pl.semaphore_signal(barrier, inc=1, device_id=((s + k) % seq_count, e), device_id_type=MESH)

    def meet(k):
        return pltpu.make_async_remote_copy(
            src_ref=top_ref, dst_ref=peaks.at[k], send_sem=m_s.at[k], recv_sem=m_r.at[k],
            device_id=((s + k) % seq_count, e), device_id_type=MESH,
        )

    def job(begin, end, first, ready, target):
        size = end - begin
        here = pl.ds(begin, size)
        part = pl.ds(0, size)
        acc[:, part] = jnp.zeros((heads, size, HD), jnp.float32)
        den[:, part] = jnp.zeros((heads, size, HD), jnp.float32)
        whole = first // bk
        last = jnp.minimum((first + size + 255 + bk - 1) // bk, blocks)

        def step(j, masked):
            @pl.when(j >= ready)
            def _():
                load(j).wait()

            key = pl.multiple_of(j * bk, bk)
            keys, values = kv[0, pl.ds(key, bk), :], kv[1, pl.ds(key, bk), :]
            lim = lim_ref[here, :] if masked else None
            for head in range(heads):
                q = q_ref[here, head * HD : (head + 1) * HD]
                p = jnp.exp2(masked_scores(q, keys, lim, key))
                acc[head, part] += jnp.dot(
                    p.astype(jnp.bfloat16), values, preferred_element_type=jnp.float32
                )
                den[head, part] += lane_sums(p)

        @pl.loop(0, whole)
        def _(j):
            step(j, False)

        @pl.loop(whole, last)
        def _(j):
            step(j, True)

        for head in range(heads):
            result = acc[head, part] / jnp.sum(den[head, part], axis=1, keepdims=True)
            target[here, head * HD : (head + 1) * HD] = result.astype(jnp.bfloat16)
        return jnp.maximum(ready, last)

    def back(i):
        here = pl.ds(cuts[i], cuts[i + 1] - cuts[i])
        return pltpu.make_async_remote_copy(
            src_ref=lent.at[here], dst_ref=o_ref.at[here], send_sem=o_s.at[i], recv_sem=o_r.at[i],
            device_id=(other, e), device_id_type=MESH,
        )

    used = jnp.int32(0)
    for i in range(len(cuts) - 1):
        used = job(cuts[i], cuts[i + 1], other * rows + cuts[i], used, lent)
        if i == 0:
            pl.semaphore_wait(barrier, seq_count - 1)

            @pl.loop(1, seq_count)
            def _(k):
                meet(k).start()

        back(i).start()
    used = job(half, rows, s * rows + half, used, o_ref)

    @pl.loop(used, blocks)
    def _(j):
        load(j).wait()

    highest = top_ref[...]
    for k in range(1, seq_count):
        meet(k).wait_recv()
        highest = jnp.maximum(highest, peaks[k])
    bound = jnp.max(highest[0]) * jnp.max(highest[1])
    safe_ref[0] = jnp.where(bound < SAFE * SAFE, 1, 0).astype(jnp.int32)
    for i in range(len(cuts) - 1):
        back(i).wait()

    @pl.loop(1, seq_count)
    def _(k):
        meet(k).wait_send()


def quick(query, keyval, lim, peak):
    rows, width = query.shape
    seq_count = lax.axis_size("seq")
    heads, bk = width // HD, 1024
    cuts = (0, 384, rows // 2)
    return pl.pallas_call(
        functools.partial(quick_kernel, bk, cuts),
        out_shape=(
            jax.ShapeDtypeStruct((rows, width), jnp.bfloat16),
            jax.ShapeDtypeStruct((1,), jnp.int32),
        ),
        in_specs=[
            pl.BlockSpec(memory_space=VMEM),
            pl.BlockSpec(memory_space=pl.ANY),
            pl.BlockSpec(memory_space=VMEM),
            pl.BlockSpec(memory_space=VMEM),
        ],
        out_specs=(pl.BlockSpec(memory_space=VMEM), pl.BlockSpec(memory_space=pltpu.SMEM)),
        scratch_shapes=[
            VMEM(keyval.shape, jnp.bfloat16),
            VMEM((rows // 2, width), jnp.bfloat16),
            VMEM((heads, rows // 2, HD), jnp.float32),
            VMEM((heads, rows // 2, HD), jnp.float32),
            VMEM((seq_count, 2, 8, HD), jnp.float32),
            pltpu.SemaphoreType.DMA((keyval.shape[1] // bk,)),
            pltpu.SemaphoreType.DMA((len(cuts) - 1,)),
            pltpu.SemaphoreType.DMA((len(cuts) - 1,)),
            pltpu.SemaphoreType.DMA((seq_count,)),
            pltpu.SemaphoreType.DMA((seq_count,)),
        ],
        compiler_params=pltpu.CompilerParams(
            collective_id=1, has_side_effects=True, vmem_limit_bytes=56 << 20
        ),
    )(query, keyval, lim, peak)


def careful_kernel(bq, bk, off_ref, q_ref, kv_ref, lim_ref, o_ref, acc, den, top):
    heads = q_ref.shape[1] // HD

    @pl.loop(0, q_ref.shape[0] // bq)
    def _(tile):
        row = pl.multiple_of(tile * bq, bq)
        acc[...] = jnp.zeros_like(acc)
        den[...] = jnp.zeros_like(den)
        top[...] = jnp.full_like(top, NEG)
        last = jnp.minimum(pl.cdiv(off_ref[0] + row + bq + 255, bk), kv_ref.shape[1] // bk)

        @pl.loop(0, last)
        def _(j):
            key = pl.multiple_of(j * bk, bk)
            keys, values = kv_ref[0, pl.ds(key, bk), :], kv_ref[1, pl.ds(key, bk), :]
            for head in range(heads):
                q = q_ref[pl.ds(row, bq), head * HD : (head + 1) * HD]
                s = masked_scores(q, keys, lim_ref[pl.ds(row, bq), :], key)
                old = top[head]
                new = jnp.maximum(old, jnp.max(s, axis=1, keepdims=True))
                top[head] = new
                p = jnp.exp2(s - new)
                shrink = jnp.exp2(old - new)
                acc[head] = acc[head] * shrink + jnp.dot(
                    p.astype(jnp.bfloat16), values, preferred_element_type=jnp.float32
                )
                den[head] = den[head] * shrink + lane_sums(p)

        for head in range(heads):
            result = acc[head] / jnp.sum(den[head], axis=1, keepdims=True)
            o_ref[pl.ds(row, bq), head * HD : (head + 1) * HD] = result.astype(jnp.bfloat16)


def careful(query, keyval, lim):
    rows, width = query.shape
    half, heads, bq, bk = rows // 2, width // HD, 128, 512
    seq_count = lax.axis_size("seq")
    mine = (lax.axis_index("seq") * rows).astype(jnp.int32)
    theirs = (seq_count - 1) * rows - mine

    def attend(q0, part):
        return pl.pallas_call(
            functools.partial(careful_kernel, bq, bk),
            out_shape=jax.ShapeDtypeStruct((half, width), jnp.bfloat16),
            grid=(1,),
            in_specs=[
                pl.BlockSpec(memory_space=pltpu.SMEM),
                pl.BlockSpec((half, width), lambda i: (part, 0)),
                pl.BlockSpec(memory_space=VMEM),
                pl.BlockSpec((half, HD), lambda i: (part, 0)),
            ],
            out_specs=pl.BlockSpec(memory_space=VMEM),
            scratch_shapes=[
                VMEM((heads, bq, HD), jnp.float32),
                VMEM((heads, bq, HD), jnp.float32),
                VMEM((heads, bq, 1), jnp.float32),
            ],
            compiler_params=pltpu.CompilerParams(vmem_limit_bytes=56 << 20),
        )(q0.reshape(1), query, keyval, lim)

    lent = attend(theirs, 0)
    back = lax.ppermute(lent, "seq", [(i, seq_count - 1 - i) for i in range(seq_count)])
    return jnp.concatenate((back, attend(mine + half, 1)), axis=0)


def per_device(text, visual, gain, w_query, w_keyval, image_count, text_gap):
    query, keyval, lim, peak = project(
        text, visual, gain, w_query, w_keyval, image_count, text_gap
    )
    attended, safe = quick(query, keyval, lim, peak)
    return lax.cond(
        safe[0] > 0,
        lambda done, *rest: done,
        lambda done, *rest: careful(*rest),
        attended, query, keyval, lim,
    )


def solution(mesh):
    in_specs = (
        P("seq", "enc"),
        P(("seq", "enc"), None),
        P("enc"),
        P("enc", None),
        P("enc", None),
        P(),
        P(),
    )
    out_specs = P("seq", "enc")
    return jax.shard_map(
        per_device, mesh=mesh, in_specs=in_specs, out_specs=out_specs, check_vma=False
    )
```
